32 devices in a mesh: segment: 4 (over z), expert: 2 (over y), dp: 4 (over x, core).
Axes of the slice: x: 2, y: 2, z: 4, core: 2. Of those that a mesh axis runs over, the one named last changes fastest.
Arguments:
- state_in: bfloat16 [4, 4, 1024, 2048], P('segment', None, ('expert', 'dp')), may hold values from -6 to 6
- entering: bfloat16 [1, 4, 1024, 2048], P(None, None, ('expert', 'dp')), may hold values from -6 to 6
- saved: bfloat16 [4, 2, 2, 1024, 2048], P('segment', None, None, ('expert', 'dp')), may hold values from -6 to 6
- route_ids: int32 [4, 2, 4, 2, 1024, 6], P('segment', None, None, None, ('expert', 'dp')), may hold values from 0 to 63, as said below
- gate_vals: float32 [4, 2, 4, 2, 1024, 6], P('segment', None, None, None, ('expert', 'dp')), may hold values from 0.25 to 1
- w_gate: bfloat16 [4, 2, 2048, 1408], P('segment', 'expert', None, 'dp'), may hold values from -0.125 to 0.125
- w_up: bfloat16 [4, 2, 2048, 1408], P('segment', 'expert', None, 'dp'), may hold values from -0.125 to 0.125
- w_down: bfloat16 [4, 2, 1408, 2048], P('segment', 'expert', 'dp'), may hold values from -0.15625 to 0.15625
- gains: float32 [4, 2, 2048], P('segment'), may hold values from 0.5 to 2
Outputs:
- state_out: bfloat16 [4, 4, 1024, 2048], P('segment', None, ('expert', 'dp'))
The draws below stay inside these ranges and needn't reach their ends.
Inputs may be any that keep to these rules, and one draw needn't show every extreme that they name: `route_ids`: the ids of one token are distinct, and a token names at most one id under 1. Within each block of 128 consecutive tokens (the tokens of one device) an id under 1 is named by at most 8 tokens. For every section, slot, unit and sublayer some id under 1 is named by exactly 8 tokens in every block, and every block has an id under 1 named by exactly 8 of its tokens.
All inputs are finite; a program needn't handle non-finite values.
Results may differ from the reference program's by a relative error of at most 0.017.
Values may be sent and summed in bfloat16 or wider, within the bound.
A program may use at most 128 MiB of HBM per device.

```python
import math
import jax
import jax.numpy as jnp
from jax import lax

D = 2048
FF = 1408
ROUTED = 64
TOPK = 6
TOK = 128
CAP = 8
SLOTS = 2
EXPERTS = 1
FFQ = 352
TOKENS = 1024
SEGMENTS = 4
N_DP = 4


def draw_route_ids(key, part):
    leading = SEGMENTS * SLOTS * 4 * 2
    blocks = TOKENS // TOK
    subkeys = jax.random.split(jax.random.fold_in(key, 11), 6)
    counts = jax.random.randint(subkeys[0], (leading, blocks, EXPERTS), 0, CAP + 1)
    busiest = jax.random.randint(subkeys[1], (leading, 1, 1), 0, EXPERTS)
    second = jax.random.randint(subkeys[2], (leading, blocks, 1), 0, EXPERTS)
    experts = jnp.arange(EXPERTS, dtype=jnp.int32)
    counts = jnp.where((experts[None, None, :] == busiest) | (experts[None, None, :] == second), CAP, counts)
    starts = jnp.cumsum(counts, axis=-1) - counts
    order_keys = jax.random.split(subkeys[3], leading * blocks)
    places = jax.vmap(lambda subkey: jax.random.permutation(subkey, TOK))(order_keys).reshape(leading, blocks, TOK)
    inside = (places[:, :, :, None] >= starts[:, :, None, :]) & (places[:, :, :, None] < (starts + counts)[:, :, None, :])
    has_route = jnp.sum(inside.astype(jnp.int32), axis=-1)
    chosen = jnp.sum(jnp.where(inside, experts, 0), axis=-1)
    others = ROUTED - EXPERTS
    scores = jax.random.randint(subkeys[4], (leading, blocks, TOK, others), 0, 1 << 20) * others + jnp.arange(others, dtype=jnp.int32)
    ignored, picked = lax.top_k(scores, TOPK)
    filler = picked.astype(jnp.int32) + EXPERTS
    column = jax.random.randint(subkeys[5], (leading, blocks, TOK, 1), 0, TOPK)
    positions = jnp.arange(TOPK, dtype=jnp.int32)
    route_ids = jnp.where((has_route[..., None] == 1) & (positions == column), chosen[..., None], filler)
    return route_ids.reshape(SEGMENTS, SLOTS, 4, 2, TOKENS, TOPK)


def shard_levels(key, dims, cuts, smallest, top_value):
    def one(position, parts):
        heights = jax.random.uniform(jax.random.fold_in(jax.random.fold_in(key, 6), position), (parts,), jnp.float32, smallest / len(cuts), top_value / len(cuts))
        return jnp.repeat(jnp.exp(heights), dims[position] // parts).reshape((-1,) + (1,) * (len(dims) - position - 1))

    loudness = one(*cuts[0])
    for cut in cuts[1:]:
        loudness = loudness * one(*cut)
    return loudness


def noise(key, extent, width, limit, cuts=(), held_as=jnp.bfloat16):
    level = shard_levels(key, extent, cuts, -0.22, 0.18) if cuts else 1.0
    values = jax.random.normal(key, extent, jnp.float32) * width * level
    return jnp.minimum(jnp.maximum(values, -limit), limit).astype(held_as)


def setup_inputs(seed: int = 0) -> dict:
    arg_keys = jax.random.split(jax.random.key(seed), 10)
    return {
        "state_in": noise(arg_keys[0], (SEGMENTS, 4, TOKENS, D), 1.0, 6.0, ((0, 4), (2, 8))),
        "entering": noise(arg_keys[1], (SLOTS - 1, 4, TOKENS, D), 1.0, 6.0, ((2, 8),)),
        "saved": noise(arg_keys[2], (SEGMENTS, SLOTS, 2, TOKENS, D), 1.0, 6.0, ((0, 4), (3, 8))),
        "route_ids": draw_route_ids(jax.random.fold_in(arg_keys[9], 71), 0),
        "gate_vals": jnp.clip(0.25 + 0.75 * jax.random.uniform(arg_keys[4], (SEGMENTS, SLOTS, 4, 2, TOKENS, TOPK), jnp.float32) ** shard_levels(arg_keys[4], (SEGMENTS, SLOTS, 4, 2, TOKENS, TOPK), ((0, 4), (4, 8)), -0.2, 0.2), 0.25, 1.0),
        "w_gate": noise(arg_keys[5], (SEGMENTS, 2 * EXPERTS, D, FF), D ** -0.5, 0.125, ((0, 4), (1, 2), (3, 4))),
        "w_up": noise(arg_keys[6], (SEGMENTS, 2 * EXPERTS, D, FF), D ** -0.5, 0.125, ((0, 4), (1, 2), (3, 4))),
        "w_down": noise(arg_keys[7], (SEGMENTS, 2 * EXPERTS, FF, D), FF ** -0.5, 0.15625, ((0, 4), (1, 2), (2, 4))),
        "gains": jnp.clip(jnp.exp(math.log(2.0) - 1.3862944 * jax.random.uniform(arg_keys[8], (SEGMENTS, 2, D), jnp.float32) ** shard_levels(arg_keys[8], (SEGMENTS, 2, D), ((0, 4),), -0.2, 0.2)), 0.5, 2.0),
    }


EPSILON = 1e-06
HIGHEST = lax.Precision.HIGHEST
CONTRACT_LAST = (((1,), (1,)), ((), ()))

def route_tables(block_ids, block_gates):
    expert_range = jnp.arange(EXPERTS, dtype=jnp.int32)
    matches = block_ids[:, :, None] == expert_range[None, None, :]
    routed = lax.optimization_barrier(jnp.sum(matches.astype(jnp.int32), axis=1))
    weighting = lax.optimization_barrier(jnp.sum(jnp.where(matches, block_gates[:, :, None], jnp.zeros_like(block_gates[:, :, None])), axis=1))
    earlier = jnp.cumsum(routed, axis=0) - routed
    slot_range = jnp.arange(CAP, dtype=jnp.int32)
    chosen = (routed[:, :, None] == 1) & (earlier[:, :, None] == slot_range[None, None, :])
    row_total = block_ids.shape[0]
    selector = jnp.transpose(chosen.reshape(row_total, EXPERTS * CAP)).astype(block_gates.dtype)
    slot_gate = lax.optimization_barrier(jnp.sum(jnp.where(chosen, weighting[:, :, None], jnp.zeros_like(weighting[:, :, None])), axis=0))
    return (selector, slot_gate.reshape(EXPERTS * CAP))

def tables_of(unit_ids, unit_gates):
    blocks = TOKENS // TOK
    return jax.vmap(route_tables)(unit_ids.reshape(blocks, TOK, TOPK), unit_gates.reshape(blocks, TOK, TOPK))

def norm_rows(values, norm_gain):
    inverse_rms = lax.rsqrt(lax.optimization_barrier(jnp.mean(values * values, axis=-1, keepdims=True)) + EPSILON)
    return ((values * inverse_rms * norm_gain).astype(jnp.bfloat16), inverse_rms)

def norm_back(values, inverse_rms, norm_gain, delta, grad_normed):
    weighted = norm_gain * grad_normed
    cubed = inverse_rms * inverse_rms * inverse_rms
    return delta + inverse_rms * weighted - values * cubed * lax.optimization_barrier(jnp.sum(weighted * values, axis=-1, keepdims=True)) / values.shape[-1]

def select_rows(selector, values):
    blocks = TOKENS // TOK
    return jnp.einsum('bst,btd->bsd', selector, values.reshape(blocks, TOK, D).astype(selector.dtype), precision=HIGHEST)

def spread_rows(selector, slot_values):
    return jnp.einsum('bst,bsd->btd', selector, slot_values, precision=HIGHEST).reshape(TOKENS, D)

def expert_slice(slot_rows, expert_index):
    blocks = TOKENS // TOK
    return slot_rows.reshape(blocks, EXPERTS, CAP, D)[:, expert_index].reshape(blocks * CAP, D)

def expert_forward(hidden_rows, gate_weight, up_weight):
    gate_pre = jnp.dot(hidden_rows, gate_weight, preferred_element_type=jnp.float32)
    up_pre = jnp.dot(hidden_rows, up_weight, preferred_element_type=jnp.float32)
    return (gate_pre, up_pre)

def expert_back(grad_in_rows, gate_pre, up_pre, gate_weight, up_weight, down_weight):
    grad_act = lax.dot_general(grad_in_rows, down_weight, CONTRACT_LAST, preferred_element_type=jnp.float32)
    sigmoid_gate = jax.nn.sigmoid(gate_pre)
    grad_gate = (grad_act * up_pre * sigmoid_gate * (1.0 + gate_pre * (1.0 - sigmoid_gate))).astype(jnp.bfloat16)
    grad_up = (grad_act * gate_pre * sigmoid_gate).astype(jnp.bfloat16)
    grad_hidden = lax.dot_general(grad_gate, gate_weight, CONTRACT_LAST, preferred_element_type=jnp.float32)
    grad_hidden = grad_hidden + lax.dot_general(grad_up, up_weight, CONTRACT_LAST, preferred_element_type=jnp.float32)
    return grad_hidden.astype(jnp.bfloat16)

def sublayer(values, unit_ids, unit_gates, layer):
    gate_all, up_all, down_all, norm_gain = layer
    blocks = TOKENS // TOK
    selector, slot_gate = tables_of(unit_ids, unit_gates)
    normed, inverse_rms = norm_rows(values, norm_gain)
    slot_rows = select_rows(selector, normed).astype(jnp.bfloat16)
    outputs = []
    for expert_index in range(EXPERTS):
        hidden_rows = expert_slice(slot_rows, expert_index)
        gate_pre, up_pre = expert_forward(hidden_rows, gate_all[expert_index], up_all[expert_index])
        activation = (jax.nn.silu(gate_pre) * up_pre).astype(jnp.bfloat16)
        summed = jnp.zeros((hidden_rows.shape[0], D), jnp.float32)
        for quarter in range(N_DP):
            offset = quarter * FFQ
            partial_value = jnp.dot(activation[:, offset:offset + FFQ], down_all[expert_index, offset:offset + FFQ], preferred_element_type=jnp.float32).astype(jnp.bfloat16)
            summed = summed + lax.optimization_barrier(partial_value).astype(jnp.float32)
        outputs.append(summed.reshape(blocks, CAP, D))
    expert_out = jnp.stack(outputs, axis=1).reshape(blocks, EXPERTS * CAP, D)
    return values + spread_rows(selector, slot_gate[:, :, None] * expert_out)

def sublayer_back(values, delta, unit_ids, unit_gates, layer):
    gate_all, up_all, down_all, norm_gain = layer
    blocks = TOKENS // TOK
    selector, slot_gate = tables_of(unit_ids, unit_gates)
    normed, inverse_rms = norm_rows(values, norm_gain)
    slot_rows = select_rows(selector, normed).astype(jnp.bfloat16)
    slot_grads = (slot_gate[:, :, None] * select_rows(selector, delta)).astype(jnp.bfloat16)
    outputs = []
    for expert_index in range(EXPERTS):
        hidden_rows = expert_slice(slot_rows, expert_index)
        grad_in_rows = expert_slice(slot_grads, expert_index)
        gate_pre, up_pre = expert_forward(hidden_rows, gate_all[expert_index], up_all[expert_index])
        summed = jnp.zeros((hidden_rows.shape[0], D), jnp.float32)
        for quarter in range(N_DP):
            offset = quarter * FFQ
            partial_value = expert_back(grad_in_rows, gate_pre[:, offset:offset + FFQ], up_pre[:, offset:offset + FFQ], gate_all[expert_index][:, offset:offset + FFQ], up_all[expert_index][:, offset:offset + FFQ], down_all[expert_index, offset:offset + FFQ])
            summed = summed + lax.optimization_barrier(partial_value).astype(jnp.float32)
        outputs.append(summed.reshape(blocks, CAP, D))
    grad_normed = spread_rows(selector, jnp.stack(outputs, axis=1).reshape(blocks, EXPERTS * CAP, D))
    return norm_back(values, inverse_rms, norm_gain, delta, grad_normed)

def forward_unit(start, unit_ids, unit_gates, layers, order):
    values = start.astype(jnp.float32)
    for sub_index in order:
        values = sublayer(values, unit_ids[sub_index], unit_gates[sub_index], layers[sub_index])
    return values.astype(jnp.bfloat16)

def backward_unit(kept, incoming, unit_ids, unit_gates, layers, order):
    first_sub = order[0]
    second_sub = order[1]
    start = kept.astype(jnp.float32)
    middle = sublayer(start, unit_ids[first_sub], unit_gates[first_sub], layers[first_sub])
    grad_middle = sublayer_back(middle, incoming.astype(jnp.float32), unit_ids[second_sub], unit_gates[second_sub], layers[second_sub])
    grad_start = sublayer_back(start, grad_middle, unit_ids[first_sub], unit_gates[first_sub], layers[first_sub])
    return grad_start.astype(jnp.bfloat16)

def reference(state_in, entering, saved, route_ids, gate_vals, w_gate, w_up, w_down, gains):
    current = state_in
    result = state_in
    for slot_index in range(SLOTS):
        produced = []
        for segment_index in range(SEGMENTS):
            layers = [(w_gate[segment_index, sub_index * EXPERTS:(sub_index + 1) * EXPERTS], w_up[segment_index, sub_index * EXPERTS:(sub_index + 1) * EXPERTS], w_down[segment_index, sub_index * EXPERTS:(sub_index + 1) * EXPERTS], gains[segment_index, sub_index]) for sub_index in range(2)]
            ids_here = route_ids[segment_index, slot_index]
            gates_here = gate_vals[segment_index, slot_index]
            first_forward = forward_unit(current[segment_index, 0], ids_here[0], gates_here[0], layers, (0, 1))
            second_forward = forward_unit(current[segment_index, 1], ids_here[1], gates_here[1], layers, (1, 0))
            first_backward = backward_unit(saved[segment_index, slot_index, 0], current[segment_index, 2], ids_here[2], gates_here[2], layers, (0, 1))
            second_backward = backward_unit(saved[segment_index, slot_index, 1], current[segment_index, 3], ids_here[3], gates_here[3], layers, (1, 0))
            produced.append(jnp.stack([first_forward, second_forward, first_backward, second_backward]))
        result = jnp.stack(produced)
        if slot_index + 1 < SLOTS:
            arriving = entering[slot_index]
            acts_up = jnp.concatenate([arriving[0][None], result[:-1, 0]], axis=0)
            acts_down = jnp.concatenate([result[1:, 1], arriving[1][None]], axis=0)
            grads_down = jnp.concatenate([result[1:, 2], arriving[2][None]], axis=0)
            grads_up = jnp.concatenate([arriving[3][None], result[:-1, 3]], axis=0)
            current = jnp.stack([acts_up, acts_down, grads_down, grads_up], axis=1)
    return result
```

```python
import functools
import jax
import jax.numpy as jnp
from jax import lax
from jax.experimental import pallas as pl
from jax.experimental.pallas import tpu as pltpu
from jax.sharding import PartitionSpec as P

CAP = 8
EPSILON = 1e-06
LAST = (((1,), (1,)), ((), ()))
MESH = pl.DeviceIdType.MESH
BF = jnp.bfloat16
F32 = jnp.float32
OUT = ("k0a", "f00", "d0b", "k1a", "k0b", "f01", "k1b", "d0a", "f10", "d1b", "f11", "d1a")
BACK = ("k0a", "f00", "k1a", "d0b", "f01", "d0a", "f10", "d1b", "f11", "d1a")
VALS = ("fx1", "fx2", "k0a", "k0b", "k1a", "k1b", "d0a", "d0b", "d1a", "d1b")
INVS = ("0a", "0b", "1a", "1b")
PRES = ("k0a", "k0b", "k1a", "k1b")
STREAMS = range(2)


def mm(a, b):
    return jnp.dot(a, b, preferred_element_type=F32)


def mm_t(a, b):
    return lax.dot_general(a, b, LAST, preferred_element_type=F32)


def mix(picks, rows):
    high = rows.astype(BF).astype(F32)
    rest = rows - high
    mid = rest.astype(BF).astype(F32)
    parts = jnp.concatenate([high, mid, rest - mid])
    return mm(picks.astype(BF), parts.astype(BF))


def unit_norm(rows, gain):
    inv = lax.rsqrt(jnp.mean(rows * rows, axis=-1, keepdims=True) + EPSILON)
    return rows * inv * gain, inv


def back_norm(rows, inv, gain, grad):
    weighted = gain * grad
    total = jnp.sum(weighted * rows, axis=-1, keepdims=True)
    return inv * weighted - rows * (inv * inv * inv) * total / rows.shape[-1]


def quotient(a, b):
    return a // b if isinstance(a, int) else lax.div(a, b)


def remainder(a, b):
    return a % b if isinstance(a, int) else lax.rem(a, b)


def kernel(sizes, state_in, entering, saved_in, ids, gates, wg_in, wu_in, wd_in, gains,
           pre_out, rows_out, spread_out,
           outs, ins, bouts, bins, base, final, state, saved, patch_out, patch_in, held_out, held_in,
           sel, gate_col, overlaps, moves, fresh_base, vals, invs, pre, early, wg, wu, wd,
           send_sem, recv_sem, local_sem, relay_send, relay_recv, enter_sem, weight_sem,
           pair_send, pair_recv, input_sem, pre_sem):
    ns, ne, nd = sizes
    nh = nd // 2
    group = ne * nh
    ec = ne // 2
    width = ec * CAP
    tokens, model = state_in.shape[1], state_in.shape[2]
    hidden = wg_in.shape[0]
    seg, ex, dp = lax.axis_index("segment"), lax.axis_index("expert"), lax.axis_index("dp")
    half, side = lax.div(dp, 2), lax.rem(dp, 2)
    me = ex * nh + half

    saved_copies = [pltpu.make_async_copy(saved_in.at[s], saved.at[s], input_sem.at[s]) for s in range(2)]
    state_copies = [
        pltpu.make_async_copy(state_in.at[pl.ds(2 * i, 2)], state.at[pl.ds(2 * i, 2)], input_sem.at[2 + i])
        for i in range(2)
    ]
    for copy in (saved_copies[0], state_copies[0], state_copies[1]):
        copy.start()

    barrier = pltpu.get_barrier_semaphore()

    def each_peer(body):
        if group <= 8:
            for k in reversed(range(1, group)):
                body(k)
        else:
            pl.loop(1, group)(body)

    def peer(k):
        te = lax.rem(ex + quotient(k, nh), ne)
        th = lax.rem(half + remainder(k, nh), nh)
        return te, th, (seg, te, th * 2 + side)

    def source_of(k):
        te = lax.rem(ex - quotient(k, nh) + ne, ne)
        th = lax.rem(half - remainder(k, nh) + nh, nh)
        return te * nh + th

    partner = (seg, ex, half * 2 + 1 - side)
    has_up, has_down = seg < ns - 1, seg > 0

    def greet(k):
        pl.semaphore_signal(barrier, inc=1, device_id=peer(k)[2], device_id_type=MESH)

    each_peer(greet)
    pl.semaphore_signal(barrier, inc=1, device_id=partner, device_id_type=MESH)

    @pl.when(has_up)
    def _():
        pl.semaphore_signal(barrier, inc=1, device_id=(seg + 1, ex, dp), device_id_type=MESH)

    @pl.when(has_down)
    def _():
        pl.semaphore_signal(barrier, inc=1, device_id=(seg - 1, ex, dp), device_id_type=MESH)

    weights = ((wg_in, wg), (wu_in, wu), (wd_in, wd))
    weight_copies = [
        pltpu.make_async_copy(source, dest.at[pl.ds(0, hidden)], weight_sem.at[i])
        for i, (source, dest) in enumerate(weights)
    ]
    pair_copies = [
        pltpu.make_async_remote_copy(
            src_ref=source, dst_ref=dest.at[pl.ds(hidden, hidden)], send_sem=pair_send.at[i],
            recv_sem=pair_recv.at[i], device_id=partner, device_id_type=MESH,
        )
        for i, (source, dest) in enumerate(weights)
    ]
    for copy in weight_copies:
        copy.start()
    saved_copies[1].start()

    units = state_in.shape[0]
    lane = lax.broadcasted_iota(jnp.int32, (tokens, tokens), 1)
    row = lax.broadcasted_iota(jnp.int32, (tokens, tokens), 0)
    before = (row < lane).astype(F32).astype(BF)
    eye = (row == lane).astype(F32)
    slot_row = lax.broadcasted_iota(jnp.int32, (CAP, tokens), 0).astype(F32)
    su = 2 * units
    topk = ids.shape[0] // (2 * su)

    def tab(slot, unit, sub):
        return sub * su + slot * units + unit

    for e in range(ec):
        routed, weight = [], []
        for j in range(2):
            count, total = jnp.zeros((su, tokens), F32), jnp.zeros((su, tokens), F32)
            for k in range(topk):
                rows = pl.ds(k * 2 + j, su, stride=2 * topk)
                match = ids[rows, :] == e
                count = count + match.astype(F32)
                total = total + jnp.where(match, gates[rows, :], 0.0)
            routed.append(count)
            weight.append(total)
        routed = jnp.concatenate(routed)
        weight = jnp.concatenate(weight)
        earlier = mm(routed.astype(BF), before)
        for tb in range(2 * su):
            hit = (routed[tb:tb + 1] == 1.0) & (earlier[tb:tb + 1] == slot_row)
            one = jnp.where(hit, 1.0, 0.0)
            sel[tb, e * CAP:(e + 1) * CAP] = one
            gate_col[tb, e * CAP:(e + 1) * CAP] = jnp.broadcast_to(
                jnp.sum(one * weight[tb:tb + 1], axis=1, keepdims=True), (CAP, tokens)
            )

    neighbours = jnp.where(has_up, 1, 0) + jnp.where(has_down, 1, 0)
    pl.semaphore_wait(barrier, group + neighbours)
    for copy in pair_copies:
        copy.start()

    def first_second(slot, unit):
        first = unit % 2
        return sel[tab(slot, unit, first)], sel[tab(slot, unit, 1 - first)]

    def last_picks(slot, unit):
        s1, s2 = first_second(slot, unit)
        if unit < 2:
            s1 = s1 * (1.0 - jnp.sum(s2, axis=0, keepdims=True))
        else:
            s2 = s2 * (1.0 - jnp.sum(s1, axis=0, keepdims=True))
        return jnp.concatenate([s1, s2])

    def both_picks(slot, unit):
        return jnp.concatenate(first_second(slot, unit))

    def pick(slot, unit, values):
        return mm(both_picks(slot, unit).astype(BF), values)

    def gate(slot, unit, second):
        sub = 1 - unit % 2 if second else unit % 2
        return gate_col[tab(slot, unit, sub)][:, 0:1]

    def gain(unit, second):
        sub = 1 - unit % 2 if second else unit % 2
        return gains[sub:sub + 1]

    def relay(unit, kind, source, dest):
        up = unit in (0, 3)
        goes, comes = (has_up, has_down) if up else (has_down, has_up)
        target = lax.rem(seg + (1 if up else ns - 1), ns)
        copy = pltpu.make_async_remote_copy(
            src_ref=source, dst_ref=dest, send_sem=relay_send.at[kind, unit],
            recv_sem=relay_recv.at[kind, unit], device_id=(target, ex, dp), device_id_type=MESH,
        )
        return goes, comes, copy

    def start_if(triple):
        @pl.when(triple[0])
        def _():
            triple[2].start()

    def arrive_if(triple):
        @pl.when(triple[1])
        def _():
            triple[2].wait_recv()

    bulk = [relay(u, 0, state_in.at[u], base.at[u]) for u in range(4)]
    enter = [pltpu.make_async_copy(entering.at[u], base.at[u], enter_sem.at[u]) for u in range(4)]
    patches = [relay(u, 1, patch_out.at[u], patch_in.at[u]) for u in range(4)]
    helds = [relay(u, 2, held_out.at[u], held_in.at[u]) for u in range(4)]

    def wait_bulk(u):
        arrive_if(bulk[u])

        @pl.when(jnp.logical_not(bulk[u][1]))
        def _():
            enter[u].wait()

    def out_copy(name, k):
        i = OUT.index(name)
        te, th, device = peer(k)
        return pltpu.make_async_remote_copy(
            src_ref=outs.at[i, te], dst_ref=ins.at[i, me], send_sem=send_sem.at[i, k],
            recv_sem=recv_sem.at[i, k], device_id=device, device_id_type=MESH,
        )

    def back_copy(name, k):
        i = BACK.index(name)
        te, th, device = peer(k)
        return pltpu.make_async_remote_copy(
            src_ref=bouts.at[i, te * nh + th], dst_ref=bins.at[i, me], send_sem=send_sem.at[len(OUT) + i, k],
            recv_sem=recv_sem.at[len(OUT) + i, k], device_id=device, device_id_type=MESH,
        )

    def own_out(name):
        i = OUT.index(name)
        return pltpu.make_async_copy(outs.at[i, ex], ins.at[i, me], local_sem.at[i])

    def own_back(name):
        i = BACK.index(name)
        return pltpu.make_async_copy(bouts.at[i, me], bins.at[i, me], local_sem.at[len(OUT) + i])

    def send_out(name):
        each_peer(lambda k: out_copy(name, k).start())
        own_out(name).start()

    def send_back(name):
        each_peer(lambda k: back_copy(name, k).start())
        own_back(name).start()

    def arrived(buffer, i, phase):
        def body(k):
            slot = buffer.at[i, source_of(k)]
            pltpu.make_async_remote_copy(
                src_ref=slot, dst_ref=slot, send_sem=send_sem.at[phase, k],
                recv_sem=recv_sem.at[phase, k], device_id=peer(k)[2], device_id_type=MESH,
            ).wait_recv()

        each_peer(body)

    def take_out(name):
        i = OUT.index(name)
        own_out(name).wait()
        arrived(ins, i, i)

    def take_back(name):
        i = BACK.index(name)
        own_back(name).wait()
        arrived(bins, i, len(OUT) + i)

    def put(name, unit, second, rows):
        j = 1 - unit % 2 if second else unit % 2
        for e in range(ec):
            outs[OUT.index(name), j * ec + e] = rows[e * CAP:(e + 1) * CAP].astype(BF)

    def got(name, unit, second):
        j = 1 - unit % 2 if second else unit % 2
        i = BACK.index(name)
        parts = []
        for e in range(ec):
            first = (j * ec + e) * nh
            total = bins[i, first].astype(F32)
            for q in range(1, nh):
                total = total + bins[i, first + q].astype(F32)
            parts.append(total)
        return parts[0] if ec == 1 else jnp.concatenate(parts)

    def rows_of(name):
        return ins[OUT.index(name)].astype(F32).reshape(group * CAP, model).astype(BF)

    def give(name, rows):
        bouts[BACK.index(name)] = rows.reshape(group, CAP, model).astype(BF)

    def half_forward(rows):
        return mm_t(rows, wg[...]), mm_t(rows, wu[...])

    def finish_forward(gp, up):
        return mm((gp * jax.nn.sigmoid(gp) * up).astype(BF), wd[...])

    def backward(act, gp, up):
        sig = jax.nn.sigmoid(gp)
        grad_gate = (act * up * sig * (1.0 + gp * (1.0 - sig))).astype(BF)
        grad_up = (act * gp * sig).astype(BF)
        return mm(grad_gate, wg[...]) + mm(grad_up, wu[...])

    def at(name, st):
        return VALS.index(name) * 2 + st

    def inv_at(slot, which, st):
        return INVS.index(f"{slot}{which}") * 2 + st

    def keep_inv(slot, which, st, inv):
        invs[inv_at(slot, which, st)] = jnp.broadcast_to(inv, (width, tokens))

    def held_inv(slot, which, st):
        return invs[inv_at(slot, which, st)][:, 0:1]

    def pre_at(name):
        i = PRES.index(name) * 2
        return pre[i], pre[i + 1]

    def keep_pre(name, values):
        i = PRES.index(name) * 2
        pre[i], pre[i + 1] = values

    def crossing(slot, unit, transposed):
        s1, s2 = first_second(slot, unit)
        if transposed:
            s1, s2 = s2, s1
        return mm_t(s2.astype(BF), jnp.concatenate([s1, s1, s1]).astype(BF))

    def over_at(slot, unit, transposed):
        return slot * 6 + unit + (2 if transposed else 0)

    def start_kept(slot):
        name = f"k{slot}a"
        saved_copies[slot].wait()
        for st in STREAMS:
            b = 2 + st
            both = pick(slot, b, saved[slot, st])
            vals[at(f"k{slot}a", st)], vals[at(f"k{slot}b", st)] = both[:width], both[width:]
            rows, inv = unit_norm(both[:width], gain(b, False))
            put(name, b, False, rows)
            keep_inv(slot, "a", st, inv)
        send_out(name)

    def middle_kept(slot):
        take_back(f"k{slot}a")
        for st in STREAMS:
            b = 2 + st
            add = gate(slot, b, False) * got(f"k{slot}a", b, False)
            middle = vals[at(f"k{slot}b", st)] + mix(overlaps[over_at(slot, b, False)], add)
            vals[at(f"k{slot}b", st)] = middle
            rows, inv = unit_norm(middle, gain(b, True))
            put(f"k{slot}b", b, True, rows)
            keep_inv(slot, "b", st, inv)
        send_out(f"k{slot}b")

    def forward_start(slot, st, first, second):
        vals[at("fx1", st)], vals[at("fx2", st)] = first, second
        put(f"f{slot}0", st, False, unit_norm(first, gain(st, False))[0])

    def forward_middle(slot):
        take_back(f"f{slot}0")
        for st in STREAMS:
            add = gate(slot, st, False) * got(f"f{slot}0", st, False)
            vals[at("fx1", st)] = vals[at("fx1", st)] + add
            middle = vals[at("fx2", st)] + mix(overlaps[over_at(slot, st, False)], add)
            vals[at("fx2", st)] = middle
            put(f"f{slot}1", st, True, unit_norm(middle, gain(st, True))[0])
        send_out(f"f{slot}1")

    def forward_end(slot, st, dest):
        second = vals[at("fx2", st)] + gate(slot, st, True) * got(f"f{slot}1", st, True)
        dest[st] = jnp.concatenate([vals[at("fx1", st)], second]).astype(BF)

    def backward_start(slot, st, first, second):
        vals[at(f"d{slot}a", st)], vals[at(f"d{slot}b", st)] = first, second
        put(f"d{slot}b", 2 + st, True, gate(slot, 2 + st, True) * second)

    def backward_middle(slot):
        take_back(f"d{slot}b")
        for st in STREAMS:
            b = 2 + st
            step = back_norm(
                vals[at(f"k{slot}b", st)], held_inv(slot, "b", st), gain(b, True), got(f"d{slot}b", b, True)
            )
            inner = vals[at(f"d{slot}a", st)] + mix(overlaps[over_at(slot, b, True)], step)
            put(f"d{slot}a", b, False, gate(slot, b, False) * inner)
            vals[at(f"d{slot}b", st)] = vals[at(f"d{slot}b", st)] + step
            vals[at(f"d{slot}a", st)] = inner
        send_out(f"d{slot}a")

    def backward_end(slot, st, dest):
        b = 2 + st
        first = vals[at(f"d{slot}a", st)] + back_norm(
            vals[at(f"k{slot}a", st)], held_inv(slot, "a", st), gain(b, False), got(f"d{slot}a", b, False)
        )
        dest[b] = jnp.concatenate([first, vals[at(f"d{slot}b", st)]]).astype(BF)

    def expert_forward(name, kept=False):
        take_out(name)
        gp, up = half_forward(rows_of(name))
        if kept:
            keep_pre(name, (gp, up))
        give(name, finish_forward(gp, up))
        send_back(name)

    def expert_backward(name, pres):
        take_out(name)
        give(name, backward(mm_t(rows_of(name), wd[...]), *pre_at(pres)))
        send_back(name)

    def ready_unit(u):
        wait_bulk(u)
        arrive_if(helds[u])
        held = held_in[u].astype(F32)
        both = both_picks(1, u)
        keep = 1.0 - jnp.sum(held, axis=0, keepdims=True)
        moves[u] = mm_t(both.astype(BF), held.astype(BF))
        fresh_base[u] = mm((both * keep).astype(BF), base[u])

    def pick_new(u):
        arrive_if(patches[u])
        return fresh_base[u] + mm(moves[u].astype(BF), patch_in[u])

    pre_copies = [pltpu.make_async_copy(final.at[u], pre_out.at[u], pre_sem.at[u]) for u in range(4)]

    def settle(u):
        new_sel = last_picks(1, u)
        fresh = 1.0 - jnp.sum(new_sel, axis=0, keepdims=True)
        old_sel = held_in[u].astype(F32) * fresh
        kept = eye * (fresh - jnp.sum(old_sel, axis=0, keepdims=True))
        spread = mm_t(eye.astype(BF), jnp.concatenate([old_sel, new_sel]).astype(BF))
        spread_out[u] = spread[:, 2 * width:].astype(BF)
        final[u] = (mm(kept.astype(BF), base[u]) + mm(spread[:, :2 * width].astype(BF), patch_in[u])).astype(BF)
        pre_copies[u].start()

    start_kept(0)
    state_copies[0].wait()
    for st in STREAMS:
        both = pick(0, st, state[st])
        forward_start(0, st, both[:width], both[width:])
    send_out("f00")
    state_copies[1].wait()
    for st in STREAMS:
        both = pick(0, 2 + st, state[2 + st])
        backward_start(0, st, both[:width], both[width:])
    send_out("d0b")

    for u in range(4):
        held_out[u] = last_picks(0, u).astype(BF)
    for u in range(4):
        start_if(helds[u])

        @pl.when(jnp.logical_not(helds[u][1]))
        def _(u=u):
            patch_in[u] = jnp.zeros(patch_in.shape[1:], BF)
            held_in[u] = jnp.zeros(held_in.shape[1:], BF)
    for u in range(4):
        start_if(bulk[u])

        @pl.when(jnp.logical_not(bulk[u][1]))
        def _(u=u):
            enter[u].start()
    for slot in range(2):
        for u in range(4):
            overlaps[over_at(slot, u, False)] = crossing(slot, u, False)
            if u >= 2:
                overlaps[over_at(slot, u, True)] = crossing(slot, u, True)

    for i in range(3):
        weight_copies[i].wait()
        pair_copies[i].wait_recv()
    expert_forward("k0a", True)
    expert_forward("f00")
    start_kept(1)
    take_out("d0b")
    early[...] = mm_t(rows_of("d0b"), wd[...])
    middle_kept(0)
    forward_middle(0)
    expert_forward("k1a", True)
    take_out("k0b")
    give("d0b", backward(early[...], *half_forward(rows_of("k0b"))))
    send_back("d0b")
    expert_forward("f01")
    middle_kept(1)
    backward_middle(0)
    take_back("f01")
    for st in STREAMS:
        forward_end(0, st, patch_out)
    for st in STREAMS:
        start_if(patches[st])
    take_out("k1b")
    keep_pre("k1b", half_forward(rows_of("k1b")))
    expert_backward("d0a", "k0a")
    for st in STREAMS:
        ready_unit(st)
    for st in STREAMS:
        both = pick_new(st)
        forward_start(1, st, both[:width], both[width:])
    send_out("f10")
    take_back("d0a")
    for st in STREAMS:
        backward_end(0, st, patch_out)
    for st in STREAMS:
        start_if(patches[2 + st])
    for st in STREAMS:
        ready_unit(2 + st)
    expert_forward("f10")
    for st in STREAMS:
        both = pick_new(2 + st)
        backward_start(1, st, both[:width], both[width:])
    send_out("d1b")
    forward_middle(1)
    for u in range(4):
        settle(u)
    expert_backward("d1b", "k1b")
    expert_forward("f11")
    backward_middle(1)
    take_back("f11")
    for st in STREAMS:
        forward_end(1, st, rows_out)
    expert_backward("d1a", "k1a")
    take_back("d1a")
    for st in STREAMS:
        backward_end(1, st, rows_out)

    for copy in pre_copies:
        copy.wait()
    for name in OUT:
        each_peer(lambda k, name=name: out_copy(name, k).wait_send())
    for name in BACK:
        each_peer(lambda k, name=name: back_copy(name, k).wait_send())
    for copy in pair_copies:
        copy.wait_send()
    for triple in bulk + patches + helds:
        @pl.when(triple[0])
        def _(triple=triple):
            triple[2].wait_send()


def merge(pre, rows, spread, out):
    out[0] = (pre[0].astype(F32) + mm(spread[0], rows[0])).astype(BF)


def local(sizes, state_in, entering, saved, route_ids, gate_vals, w_gate, w_up, w_down, gains):
    ns, ne, nd = sizes
    group, width = ne * nd // 2, ne // 2 * CAP
    units, tokens, model = state_in.shape[1:]
    hidden = w_gate.shape[-1]
    tables = route_ids.shape[1] * route_ids.shape[2] * route_ids.shape[3]
    topk = route_ids.shape[-1]
    turn = (0, 1, 2, 5, 3, 4)
    ids = jnp.transpose(route_ids, turn).reshape(tables * topk, tokens)
    gates = jnp.transpose(gate_vals, turn).reshape(tables * topk, tokens)
    vmem = pl.BlockSpec(memory_space=pltpu.VMEM)
    anywhere = pl.BlockSpec(memory_space=pl.ANY)
    dma = pltpu.SemaphoreType.DMA
    phases = len(OUT) + len(BACK)
    scratch = [
        pltpu.VMEM((len(OUT), ne, CAP, model), BF),
        pltpu.VMEM((len(OUT), group, CAP, model), BF),
        pltpu.VMEM((len(BACK), group, CAP, model), BF),
        pltpu.VMEM((len(BACK), group, CAP, model), BF),
        pltpu.VMEM((units, tokens, model), BF),
        pltpu.VMEM((units, tokens, model), BF),
        pltpu.VMEM((units, tokens, model), BF),
        pltpu.VMEM(saved.shape[1:], BF),
        pltpu.VMEM((units, 2 * width, model), BF),
        pltpu.VMEM((units, 2 * width, model), BF),
        pltpu.VMEM((units, 2 * width, tokens), BF),
        pltpu.VMEM((units, 2 * width, tokens), BF),
        pltpu.VMEM((tables, width, tokens), F32),
        pltpu.VMEM((tables, width, tokens), F32),
        pltpu.VMEM((12, width, 3 * width), F32),
        pltpu.VMEM((units, 2 * width, 2 * width), F32),
        pltpu.VMEM((units, 2 * width, model), F32),
        pltpu.VMEM((2 * len(VALS), width, model), F32),
        pltpu.VMEM((2 * len(INVS), width, tokens), F32),
        pltpu.VMEM((2 * len(PRES), group * CAP, 2 * hidden), F32),
        pltpu.VMEM((group * CAP, 2 * hidden), F32),
        pltpu.VMEM((2 * hidden, model), BF),
        pltpu.VMEM((2 * hidden, model), BF),
        pltpu.VMEM((2 * hidden, model), BF),
        dma((phases, group)), dma((phases, group)), dma((phases,)),
        dma((3, units)), dma((3, units)), dma((units,)), dma((3,)),
        dma((3,)), dma((3,)), dma((4,)), dma((units,)),
    ]
    pre, rows, spread = pl.pallas_call(
        functools.partial(kernel, sizes),
        out_shape=(
            jax.ShapeDtypeStruct((units, tokens, model), BF),
            jax.ShapeDtypeStruct((units, 2 * width, model), BF),
            jax.ShapeDtypeStruct((units, tokens, 2 * width), BF),
        ),
        in_specs=[anywhere, anywhere, anywhere, vmem, vmem, anywhere, anywhere, anywhere, vmem],
        out_specs=(anywhere, vmem, vmem),
        scratch_shapes=scratch,
        compiler_params=pltpu.CompilerParams(
            collective_id=0, has_side_effects=True, vmem_limit_bytes=67043328
        ),
    )(state_in[0], entering[0], saved[0], ids, gates, jnp.swapaxes(w_gate[0, 0], 0, 1),
      jnp.swapaxes(w_up[0, 0], 0, 1), w_down[0, 0], gains[0])
    result = pl.pallas_call(
        merge,
        grid=(units,),
        out_shape=jax.ShapeDtypeStruct((units, tokens, model), BF),
        in_specs=[
            pl.BlockSpec((1, tokens, model), lambda u: (u, 0, 0)),
            pl.BlockSpec((1, 2 * width, model), lambda u: (u, 0, 0)),
            pl.BlockSpec((1, tokens, 2 * width), lambda u: (u, 0, 0)),
        ],
        out_specs=pl.BlockSpec((1, tokens, model), lambda u: (u, 0, 0)),
    )(pre, rows, spread)
    return result[None]


def solution(mesh):
    in_specs = (
        P("segment", None, ("expert", "dp"), None),
        P(None, None, ("expert", "dp"), None),
        P("segment", None, None, ("expert", "dp"), None),
        P("segment", None, None, None, ("expert", "dp"), None),
        P("segment", None, None, None, ("expert", "dp"), None),
        P("segment", "expert", None, "dp"),
        P("segment", "expert", None, "dp"),
        P("segment", "expert", "dp", None),
        P("segment", None, None),
    )
    out_specs = P("segment", None, ("expert", "dp"), None)
    sizes = (mesh.shape["segment"], mesh.shape["expert"], mesh.shape["dp"])
    body = functools.partial(local, sizes)
    return jax.shard_map(body, mesh=mesh, in_specs=in_specs, out_specs=out_specs, check_vma=False)
```

```python
import functools
import jax
import jax.numpy as jnp
from jax import lax
from jax.experimental import pallas as pl
from jax.experimental.pallas import tpu as pltpu
from jax.sharding import PartitionSpec as P

CAP = 8
EPSILON = 1e-06
LAST = (((1,), (1,)), ((), ()))
MESH = pl.DeviceIdType.MESH
BF = jnp.bfloat16
F32 = jnp.float32
OUT = ("k0a", "f00", "d0b", "k1a", "k0b", "f01", "k1b", "d0a", "f10", "d1b", "f11", "d1a")
BACK = ("k0a", "f00", "k1a", "d0b", "f01", "d0a", "f10", "d1b", "f11", "d1a")
VALS = ("fx1", "fx2", "k0a", "k0b", "k1a", "k1b", "d0a", "d0b", "d1a", "d1b")
INVS = ("0a", "0b", "1a", "1b")
PRES = ("k0a", "k0b", "k1a", "k1b")
STREAMS = range(2)


def mm(a, b):
    return jnp.dot(a, b, preferred_element_type=F32)


def mm_t(a, b):
    return lax.dot_general(a, b, LAST, preferred_element_type=F32)


def mm_flip(rows, weights):
    return lax.dot_general(weights, rows, LAST, preferred_element_type=F32).T


def mix(picks, rows):
    high = rows.astype(BF).astype(F32)
    rest = rows - high
    mid = rest.astype(BF).astype(F32)
    parts = jnp.concatenate([high, mid, rest - mid])
    return mm(picks.astype(BF), parts.astype(BF))


def unit_norm(rows, gain):
    inv = lax.rsqrt(jnp.mean(rows * rows, axis=-1, keepdims=True) + EPSILON)
    return rows * inv * gain, inv


def back_norm(rows, inv, gain, grad):
    weighted = gain * grad
    total = jnp.sum(weighted * rows, axis=-1, keepdims=True)
    return inv * weighted - rows * (inv * inv * inv) * total / rows.shape[-1]


def quotient(a, b):
    return a // b if isinstance(a, int) else lax.div(a, b)


def remainder(a, b):
    return a % b if isinstance(a, int) else lax.rem(a, b)


def kernel(sizes, state_in, entering, saved_in, ids_in, gates_in, wg_in, wu_in, wd_in, gains_in,
           final, rows_out, spread_out,
           outs, ins, bouts, bins, base, ids, gates, gains, state, saved, patch_out, patch_in, held_out, held_in,
           sel, gate_col, overlaps, moves, fresh_base, vals, invs, pre, early, wg, wu, wd,
           send_sem, recv_sem, relay_send, relay_recv, enter_sem, weight_sem,
           pair_send, pair_recv, input_sem, small_sem):
    ns, ne, nd = sizes
    nh = nd // 2
    group = ne * nh
    ec = ne // 2
    width = ec * CAP
    tokens, model = state_in.shape[1], state_in.shape[2]
    hidden = wg_in.shape[0]
    hm = model // 2
    gr = group * CAP
    seg, ex, dp = lax.axis_index("segment"), lax.axis_index("expert"), lax.axis_index("dp")
    half, side = lax.div(dp, 2), lax.rem(dp, 2)
    me = ex * nh + half

    saved_copies = [pltpu.make_async_copy(saved_in.at[s], saved.at[s], input_sem.at[s]) for s in range(2)]
    state_copies = [
        pltpu.make_async_copy(state_in.at[pl.ds(2 * i, 2)], state.at[pl.ds(2 * i, 2)], input_sem.at[2 + i])
        for i in range(2)
    ]
    small_copies = [
        pltpu.make_async_copy(source, dest, small_sem.at[i])
        for i, (source, dest) in enumerate(((ids_in, ids), (gates_in, gates), (gains_in, gains)))
    ]
    for copy in (*small_copies, saved_copies[0]):
        copy.start()

    barrier = pltpu.get_barrier_semaphore()

    def each_peer(body):
        if group <= 8:
            for k in reversed(range(1, group)):
                body(k)
        else:
            pl.loop(1, group)(body)

    def peer(k):
        te = lax.rem(ex + quotient(k, nh), ne)
        th = lax.rem(half + remainder(k, nh), nh)
        return te, th, (seg, te, th * 2 + 1 - side)

    partner = (seg, ex, half * 2 + 1 - side)
    has_up, has_down = seg < ns - 1, seg > 0

    def greet(k):
        pl.semaphore_signal(barrier, inc=1, device_id=peer(k)[2], device_id_type=MESH)

    each_peer(greet)
    pl.semaphore_signal(barrier, inc=1, device_id=partner, device_id_type=MESH)

    @pl.when(has_up)
    def _():
        pl.semaphore_signal(barrier, inc=1, device_id=(seg + 1, ex, dp), device_id_type=MESH)

    @pl.when(has_down)
    def _():
        pl.semaphore_signal(barrier, inc=1, device_id=(seg - 1, ex, dp), device_id_type=MESH)

    weights = ((wg_in, wg), (wu_in, wu), (wd_in, wd))
    weight_copies = [
        pltpu.make_async_copy(source, dest.at[pl.ds(0, hidden)], weight_sem.at[i])
        for i, (source, dest) in enumerate(weights)
    ]
    pair_copies = [
        pltpu.make_async_remote_copy(
            src_ref=source, dst_ref=dest.at[pl.ds(hidden, hidden)], send_sem=pair_send.at[i],
            recv_sem=pair_recv.at[i], device_id=partner, device_id_type=MESH,
        )
        for i, (source, dest) in enumerate(weights)
    ]
    for copy in (state_copies[0], *weight_copies, saved_copies[1], state_copies[1]):
        copy.start()

    units = state_in.shape[0]
    lane = lax.broadcasted_iota(jnp.int32, (tokens, tokens), 1)
    row = lax.broadcasted_iota(jnp.int32, (tokens, tokens), 0)
    before = (row < lane).astype(F32).astype(BF)
    eye = (row == lane).astype(F32)
    slot_row = lax.broadcasted_iota(jnp.int32, (CAP, tokens), 0).astype(F32)
    su = 2 * units
    topk = ids.shape[0] // (2 * su)

    def tab(slot, unit, sub):
        return sub * su + slot * units + unit

    small_copies[0].wait()
    small_copies[1].wait()
    for e in range(ec):
        routed, weight = [], []
        for j in range(2):
            count, total = jnp.zeros((su, tokens), F32), jnp.zeros((su, tokens), F32)
            for k in range(topk):
                rows = pl.ds(k * 2 + j, su, stride=2 * topk)
                match = ids[rows, :] == e
                count = count + match.astype(F32)
                total = total + jnp.where(match, gates[rows, :], 0.0)
            routed.append(count)
            weight.append(total)
        routed = jnp.concatenate(routed)
        weight = jnp.concatenate(weight)
        earlier = mm(routed.astype(BF), before)
        for tb in range(2 * su):
            hit = (routed[tb:tb + 1] == 1.0) & (earlier[tb:tb + 1] == slot_row)
            one = jnp.where(hit, 1.0, 0.0)
            sel[tb, e * CAP:(e + 1) * CAP] = one
            gate_col[tb, e * CAP:(e + 1) * CAP] = jnp.broadcast_to(
                jnp.sum(one * weight[tb:tb + 1], axis=1, keepdims=True), (CAP, tokens)
            )

    def first_second(slot, unit):
        first = unit % 2
        return sel[tab(slot, unit, first)], sel[tab(slot, unit, 1 - first)]

    def last_picks(slot, unit):
        s1, s2 = first_second(slot, unit)
        if unit < 2:
            s1 = s1 * (1.0 - jnp.sum(s2, axis=0, keepdims=True))
        else:
            s2 = s2 * (1.0 - jnp.sum(s1, axis=0, keepdims=True))
        return jnp.concatenate([s1, s2])

    def both_picks(slot, unit):
        return jnp.concatenate(first_second(slot, unit))

    def pick(slot, unit, values):
        return mm(both_picks(slot, unit).astype(BF), values)

    def gate(slot, unit, second):
        sub = 1 - unit % 2 if second else unit % 2
        return gate_col[tab(slot, unit, sub)][:, 0:1]

    def gain(unit, second):
        sub = 1 - unit % 2 if second else unit % 2
        return gains[sub:sub + 1]

    def relay(unit, kind, source, dest):
        up = unit in (0, 3)
        goes, comes = (has_up, has_down) if up else (has_down, has_up)
        target = lax.rem(seg + (1 if up else ns - 1), ns)
        copy = pltpu.make_async_remote_copy(
            src_ref=source, dst_ref=dest, send_sem=relay_send.at[kind, 0 if up else 1],
            recv_sem=relay_recv.at[kind, unit], device_id=(target, ex, dp), device_id_type=MESH,
        )
        return goes, comes, copy

    def start_if(triple):
        @pl.when(triple[0])
        def _():
            triple[2].start()

    def arrive_if(triple):
        @pl.when(triple[1])
        def _():
            triple[2].wait_recv()

    bulk = [relay(u, 0, state_in.at[u], base.at[u]) for u in range(4)]
    enter = [pltpu.make_async_copy(entering.at[u], base.at[u], enter_sem.at[u]) for u in range(4)]
    patches = [[relay(u, 1 + i, patch_out.at[u, i], patch_in.at[u, i]) for i in range(2)] for u in range(4)]
    helds = [relay(u, 3, held_out.at[u], held_in.at[u]) for u in range(4)]

    def wait_bulk(u):
        arrive_if(bulk[u])

        @pl.when(jnp.logical_not(bulk[u][1]))
        def _():
            enter[u].wait()

    def out_copy(name, hf, k):
        i = OUT.index(name)
        te, th, device = peer(k)
        return pltpu.make_async_remote_copy(
            src_ref=outs.at[i, hf, te], dst_ref=ins.at[i, hf, me], send_sem=send_sem.at[i],
            recv_sem=recv_sem.at[i, hf], device_id=device, device_id_type=MESH,
        )

    def back_copy(name, hf, k):
        i = BACK.index(name)
        te, th, device = peer(k)
        return pltpu.make_async_remote_copy(
            src_ref=bouts.at[i, hf, te * nh + th], dst_ref=bins.at[i, hf, me], send_sem=send_sem.at[len(OUT) + i],
            recv_sem=recv_sem.at[len(OUT) + i, hf], device_id=device, device_id_type=MESH,
        )

    def send_out(name):
        i = OUT.index(name)
        for hf in range(2):
            each_peer(lambda k, hf=hf: out_copy(name, hf, k).start())
        for hf in range(2):
            pltpu.make_async_copy(outs.at[i, hf, ex], ins.at[i, hf, me], recv_sem.at[i, hf]).start()

    def send_back(name, hf):
        i = BACK.index(name)
        each_peer(lambda k: back_copy(name, hf, k).start())
        pltpu.make_async_copy(bouts.at[i, hf, me], bins.at[i, hf, me], recv_sem.at[len(OUT) + i, hf]).start()

    def take_out(name, hf):
        i = OUT.index(name)
        pltpu.make_async_copy(ins.at[i, hf], ins.at[i, hf], recv_sem.at[i, hf]).wait()

    def take_back(name):
        i = BACK.index(name)
        for hf in range(2):
            pltpu.make_async_copy(bins.at[i, hf], bins.at[i, hf], recv_sem.at[len(OUT) + i, hf]).wait()

    def put(name, unit, second, rows):
        j = 1 - unit % 2 if second else unit % 2
        for e in range(ec):
            for hf in range(2):
                outs[OUT.index(name), hf, j * ec + e] = (
                    rows[e * CAP:(e + 1) * CAP, hf * hm:(hf + 1) * hm].astype(BF)
                )

    def got(name, unit, second):
        j = 1 - unit % 2 if second else unit % 2
        i = BACK.index(name)
        parts = []
        for e in range(ec):
            first = (j * ec + e) * nh
            halves = []
            for hf in range(2):
                total = bins[i, hf, first].astype(F32)
                for q in range(1, nh):
                    total = total + bins[i, hf, first + q].astype(F32)
                halves.append(total)
            parts.append(jnp.concatenate(halves, axis=1))
        return parts[0] if ec == 1 else jnp.concatenate(parts)

    def rows_of(hf, *names):
        parts = [ins[OUT.index(name), hf].astype(F32).reshape(gr, hm) for name in names]
        return (parts[0] if len(parts) == 1 else jnp.concatenate(parts)).astype(BF)

    def give(name, hf, rows):
        bouts[BACK.index(name), hf] = rows.reshape(group, CAP, hm).astype(BF)

    def cut(weight, hf):
        return weight[:, hf * hm:(hf + 1) * hm]

    def inward(weights, *names, ready=None):
        product = mm_t if len(names) == 1 else mm_flip
        sums = [None] * len(weights)
        if ready is None:
            for hf in range(2):
                for name in names:
                    take_out(name, hf)
                rows = rows_of(hf, *names)
                for i, weight in enumerate(weights):
                    part = product(rows, cut(weight, hf))
                    sums[i] = part if hf == 0 else sums[i] + part
            return sums
        for hf in range(2):
            for name in names:
                take_out(name, hf)
        for i, weight in enumerate(weights):
            ready(i)
            sums[i] = product(rows_of(0, *names), cut(weight, 0)) + product(rows_of(1, *names), cut(weight, 1))
        return sums

    def activate(gp, up):
        return (gp * jax.nn.sigmoid(gp) * up).astype(BF)

    def outward(names, pairs):
        for hf in range(2):
            total = mm(pairs[0][0], cut(pairs[0][1], hf))
            for a, weight in pairs[1:]:
                total = total + mm(a, cut(weight, hf))
            for n, name in enumerate(names):
                give(name, hf, total[n * gr:(n + 1) * gr])
                send_back(name, hf)

    def backward(name, act, gp, up):
        sig = jax.nn.sigmoid(gp)
        grad_gate = (act * up * sig * (1.0 + gp * (1.0 - sig))).astype(BF)
        grad_up = (act * gp * sig).astype(BF)
        outward((name,), ((grad_gate, wg), (grad_up, wu)))

    def at(name, st):
        return VALS.index(name) * 2 + st

    def inv_at(slot, which, st):
        return INVS.index(f"{slot}{which}") * 2 + st

    def keep_inv(slot, which, st, inv):
        invs[inv_at(slot, which, st)] = jnp.broadcast_to(inv, (width, tokens))

    def held_inv(slot, which, st):
        return invs[inv_at(slot, which, st)][:, 0:1]

    def pre_at(name):
        i = PRES.index(name) * 2
        return pre[i], pre[i + 1]

    def keep_pre(name, values):
        i = PRES.index(name) * 2
        pre[i], pre[i + 1] = values

    def crossing(slot, unit, transposed):
        s1, s2 = first_second(slot, unit)
        if transposed:
            s1, s2 = s2, s1
        return mm_t(s2.astype(BF), jnp.concatenate([s1, s1, s1]).astype(BF))

    def over_at(slot, unit, transposed):
        return slot * 6 + unit + (2 if transposed else 0)

    def start_kept(slot):
        name = f"k{slot}a"
        saved_copies[slot].wait()
        for st in STREAMS:
            b = 2 + st
            both = pick(slot, b, saved[slot, st])
            vals[at(f"k{slot}a", st)], vals[at(f"k{slot}b", st)] = both[:width], both[width:]
            rows, inv = unit_norm(both[:width], gain(b, False))
            put(name, b, False, rows)
            keep_inv(slot, "a", st, inv)

    def middle_kept(slot):
        take_back(f"k{slot}a")
        for st in STREAMS:
            b = 2 + st
            add = gate(slot, b, False) * got(f"k{slot}a", b, False)
            middle = vals[at(f"k{slot}b", st)] + mix(overlaps[over_at(slot, b, False)], add)
            vals[at(f"k{slot}b", st)] = middle
            rows, inv = unit_norm(middle, gain(b, True))
            put(f"k{slot}b", b, True, rows)
            keep_inv(slot, "b", st, inv)
        send_out(f"k{slot}b")

    def forward_start(slot, st, first, second):
        vals[at("fx1", st)], vals[at("fx2", st)] = first, second
        put(f"f{slot}0", st, False, unit_norm(first, gain(st, False))[0])

    def send_patch(u, part, rows):
        patch_out[u, part] = rows.astype(BF)
        start_if(patches[u][part])

    def forward_middle(slot):
        take_back(f"f{slot}0")
        for st in STREAMS:
            add = gate(slot, st, False) * got(f"f{slot}0", st, False)
            vals[at("fx1", st)] = vals[at("fx1", st)] + add
            middle = vals[at("fx2", st)] + mix(overlaps[over_at(slot, st, False)], add)
            vals[at("fx2", st)] = middle
            put(f"f{slot}1", st, True, unit_norm(middle, gain(st, True))[0])
        send_out(f"f{slot}1")

    def forward_end(slot, st):
        return vals[at("fx2", st)] + gate(slot, st, True) * got(f"f{slot}1", st, True)

    def backward_start(slot, st, first, second):
        vals[at(f"d{slot}a", st)], vals[at(f"d{slot}b", st)] = first, second
        put(f"d{slot}b", 2 + st, True, gate(slot, 2 + st, True) * second)

    def backward_middle(slot):
        take_back(f"d{slot}b")
        for st in STREAMS:
            b = 2 + st
            step = back_norm(
                vals[at(f"k{slot}b", st)], held_inv(slot, "b", st), gain(b, True), got(f"d{slot}b", b, True)
            )
            inner = vals[at(f"d{slot}a", st)] + mix(overlaps[over_at(slot, b, True)], step)
            put(f"d{slot}a", b, False, gate(slot, b, False) * inner)
            vals[at(f"d{slot}b", st)] = vals[at(f"d{slot}b", st)] + step
            vals[at(f"d{slot}a", st)] = inner
        send_out(f"d{slot}a")

    def backward_end(slot, st):
        b = 2 + st
        return vals[at(f"d{slot}a", st)] + back_norm(
            vals[at(f"k{slot}a", st)], held_inv(slot, "a", st), gain(b, False), got(f"d{slot}a", b, False)
        )

    def expert_forward(name):
        gp, up = inward((wg, wu), name)
        outward((name,), ((activate(gp, up), wd),))

    def expert_backward(name, pres):
        act, = inward((wd,), name)
        backward(name, act, *pre_at(pres))

    def ready_unit(u):
        last = 1 if u < 2 else 0
        wait_bulk(u)
        arrive_if(helds[u])
        arrive_if(patches[u][1 - last])
        held = held_in[u].astype(F32)
        both = both_picks(1, u)
        keep = 1.0 - jnp.sum(held, axis=0, keepdims=True)
        parts = [mm_t(both.astype(BF), held[i * width:(i + 1) * width].astype(BF)) for i in range(2)]
        moves[u] = parts[last]
        fresh_base[u] = mm((both * keep).astype(BF), base[u]) + mm(parts[1 - last].astype(BF), patch_in[u, 1 - last])

    def pick_new(u):
        last = 1 if u < 2 else 0
        arrive_if(patches[u][last])
        return fresh_base[u] + mm(moves[u].astype(BF), patch_in[u, last])

    def settle(u, parts):
        new_sel = last_picks(1, u)
        fresh = 1.0 - jnp.sum(new_sel, axis=0, keepdims=True)
        old_sel = held_in[u].astype(F32) * fresh
        kept = eye * (fresh - jnp.sum(old_sel, axis=0, keepdims=True))
        picks = [old_sel] + [new_sel[i * width:(i + 1) * width] for i, _ in parts]
        rows = [patch_in[u, i].astype(F32) for i in range(2)] + [value for _, value in parts]
        spread = mm_t(eye.astype(BF), jnp.concatenate(picks).astype(BF))
        final[u] = (
            mm(kept.astype(BF), base[u]) + mm(spread.astype(BF), jnp.concatenate(rows).astype(BF))
        ).astype(BF)
        if u >= 2:
            spread_out[u - 2] = mm_t(eye.astype(BF), new_sel[:width].astype(BF)).astype(BF)

    def drain(*phases):
        for phase in phases:
            sent = ins.at[0, :, pl.ds(0, group - 1)]
            pltpu.make_async_copy(sent, sent, send_sem.at[phase]).wait()

    neighbours = jnp.where(has_up, 1, 0) + jnp.where(has_down, 1, 0)
    pl.semaphore_wait(barrier, group + neighbours)
    for copy in pair_copies:
        copy.start()
    small_copies[2].wait()
    start_kept(0)
    send_out("k0a")
    state_copies[0].wait()
    for st in STREAMS:
        both = pick(0, st, state[st])
        forward_start(0, st, both[:width], both[width:])
    send_out("f00")
    start_kept(1)
    send_out("k1a")
    state_copies[1].wait()
    for st in STREAMS:
        both = pick(0, 2 + st, state[2 + st])
        backward_start(0, st, both[:width], both[width:])
    send_out("d0b")

    for u in range(4):
        held_out[u] = last_picks(0, u).astype(BF)
    for u in range(4):
        start_if(helds[u])

        @pl.when(jnp.logical_not(helds[u][1]))
        def _(u=u):
            patch_in[u] = jnp.zeros(patch_in.shape[1:], BF)
            held_in[u] = jnp.zeros(held_in.shape[1:], BF)
    for u in range(4):
        start_if(bulk[u])

        @pl.when(jnp.logical_not(bulk[u][1]))
        def _(u=u):
            enter[u].start()
    for slot in range(2):
        for u in range(4):
            overlaps[over_at(slot, u, False)] = crossing(slot, u, False)
            if u >= 2:
                overlaps[over_at(slot, u, True)] = crossing(slot, u, True)

    def wait_weight(i):
        weight_copies[i].wait()
        pair_copies[i].wait_recv()

    gp, up = inward((wg, wu), "k0a", ready=wait_weight)
    keep_pre("k0a", (gp, up))
    wait_weight(2)
    outward(("k0a",), ((activate(gp, up), wd),))
    gp, up = inward((wg, wu), "f00", "k1a")
    outward(("f00", "k1a"), ((activate(gp, up), wd),))
    keep_pre("k1a", (gp[gr:], up[gr:]))
    middle_kept(0)
    forward_middle(0)
    for st in STREAMS:
        send_patch(st, 0, vals[at("fx1", st)])
    early[...], = inward((wd,), "d0b")
    middle_kept(1)
    gp, up = inward((wg, wu), "k0b")
    backward("d0b", early[...], gp, up)
    gp, up = inward((wg, wu), "f01", "k1b")
    outward(("f01",), ((activate(gp[:gr], up[:gr]), wd),))
    keep_pre("k1b", (gp[gr:], up[gr:]))
    backward_middle(0)
    for st in STREAMS:
        send_patch(2 + st, 1, vals[at("d0b", st)])
    take_back("f01")
    for st in STREAMS:
        send_patch(st, 1, forward_end(0, st))
    expert_backward("d0a", "k0a")
    for st in STREAMS:
        ready_unit(st)
    for st in STREAMS:
        both = pick_new(st)
        forward_start(1, st, both[:width], both[width:])
    send_out("f10")
    for st in STREAMS:
        ready_unit(2 + st)
    take_back("d0a")
    for st in STREAMS:
        send_patch(2 + st, 0, backward_end(0, st))
    expert_forward("f10")
    for st in STREAMS:
        both = pick_new(2 + st)
        backward_start(1, st, both[:width], both[width:])
    send_out("d1b")
    forward_middle(1)
    expert_backward("d1b", "k1b")
    expert_forward("f11")
    backward_middle(1)
    for st in STREAMS:
        settle(2 + st, [(1, vals[at("d1b", st)])])
    take_back("f11")
    for st in STREAMS:
        settle(st, [(0, vals[at("fx1", st)]), (1, forward_end(1, st))])
    expert_backward("d1a", "k1a")
    last = len(OUT) + len(BACK) - 1
    drain(*range(last))
    for copy in pair_copies:
        copy.wait_send()
    for goes, way in ((has_up, 0), (has_down, 1)):
        @pl.when(goes)
        def _(way=way):
            pairs = (base.at[pl.ds(0, 2)], patch_in.at[0], patch_in.at[0], held_in.at[pl.ds(0, 2)])
            for kind, sent in enumerate(pairs):
                pltpu.make_async_copy(sent, sent, relay_send.at[kind, way]).wait()
    take_back("d1a")
    for st in STREAMS:
        rows_out[st] = backward_end(1, st).astype(BF)
    drain(last)


def merge(final, rows, spread, out, merged, out_sem):
    units = final.shape[0]
    sources = [final.at[u] if u < 2 else merged.at[u - 2] for u in range(units)]
    copies = [pltpu.make_async_copy(sources[u], out.at[u], out_sem.at[u]) for u in range(units)]
    for u in range(units):
        if u >= 2:
            merged[u - 2] = (final[u].astype(F32) + mm(spread[u - 2], rows[u - 2])).astype(BF)
        copies[u].start()
    for copy in copies:
        copy.wait()


def stay(value):
    return pltpu.with_memory_space_constraint(value, pltpu.HBM)


def local(sizes, state_in, entering, saved, route_ids, gate_vals, w_gate, w_up, w_down, gains):
    ns, ne, nd = sizes
    group, width = ne * nd // 2, ne // 2 * CAP
    units, tokens, model = state_in.shape[1:]
    hidden = w_gate.shape[-1]
    tables = route_ids.shape[1] * route_ids.shape[2] * route_ids.shape[3]
    topk = route_ids.shape[-1]
    turn = (0, 1, 2, 5, 3, 4)
    ids = jnp.transpose(route_ids, turn).reshape(tables * topk, tokens)
    gates = jnp.transpose(gate_vals, turn).reshape(tables * topk, tokens)
    vmem = pl.BlockSpec(memory_space=pltpu.VMEM)
    anywhere = pl.BlockSpec(memory_space=pl.ANY)
    dma = pltpu.SemaphoreType.DMA
    phases = len(OUT) + len(BACK)
    scratch = [
        pltpu.VMEM((len(OUT), 2, ne, CAP, model // 2), BF),
        pltpu.VMEM((len(OUT), 2, group, CAP, model // 2), BF),
        pltpu.VMEM((len(BACK), 2, group, CAP, model // 2), BF),
        pltpu.VMEM((len(BACK), 2, group, CAP, model // 2), BF),
        pltpu.VMEM((units, tokens, model), BF),
        pltpu.VMEM(ids.shape, jnp.int32),
        pltpu.VMEM(gates.shape, F32),
        pltpu.VMEM(gains.shape[1:], F32),
        pltpu.VMEM((units, tokens, model), BF),
        pltpu.VMEM(saved.shape[1:], BF),
        pltpu.VMEM((units, 2, width, model), BF),
        pltpu.VMEM((units, 2, width, model), BF),
        pltpu.VMEM((units, 2 * width, tokens), BF),
        pltpu.VMEM((units, 2 * width, tokens), BF),
        pltpu.VMEM((tables, width, tokens), F32),
        pltpu.VMEM((tables, width, tokens), F32),
        pltpu.VMEM((12, width, 3 * width), F32),
        pltpu.VMEM((units, 2 * width, width), F32),
        pltpu.VMEM((units, 2 * width, model), F32),
        pltpu.VMEM((2 * len(VALS), width, model), F32),
        pltpu.VMEM((2 * len(INVS), width, tokens), F32),
        pltpu.VMEM((2 * len(PRES), group * CAP, 2 * hidden), F32),
        pltpu.VMEM((group * CAP, 2 * hidden), F32),
        pltpu.VMEM((2 * hidden, model), BF),
        pltpu.VMEM((2 * hidden, model), BF),
        pltpu.VMEM((2 * hidden, model), BF),
        dma((phases,)), dma((phases, 2)),
        dma((4, 2)), dma((4, units)), dma((units,)), dma((3,)),
        dma((3,)), dma((3,)), dma((4,)), dma((3,)),
    ]
    final, rows, spread = pl.pallas_call(
        functools.partial(kernel, sizes),
        out_shape=(
            jax.ShapeDtypeStruct((units, tokens, model), BF),
            jax.ShapeDtypeStruct((2, width, model), BF),
            jax.ShapeDtypeStruct((2, tokens, width), BF),
        ),
        in_specs=[anywhere] * 9,
        out_specs=(vmem, vmem, vmem),
        scratch_shapes=scratch,
        compiler_params=pltpu.CompilerParams(
            collective_id=0, has_side_effects=True, vmem_limit_bytes=(44 if ne <= 4 else 60) * 1024 * 1024
        ),
    )(*map(stay, (
        state_in[0], entering[0], saved[0], ids, gates, jnp.swapaxes(w_gate[0, 0], 0, 1),
        jnp.swapaxes(w_up[0, 0], 0, 1), w_down[0, 0], gains[0],
    )))
    result = pl.pallas_call(
        merge,
        out_shape=jax.ShapeDtypeStruct((units, tokens, model), BF),
        in_specs=[vmem] * 3,
        out_specs=pl.BlockSpec(memory_space=pltpu.HBM),
        scratch_shapes=[
            pltpu.VMEM((units - 2, tokens, model), BF), dma((units,)),
        ],
        compiler_params=pltpu.CompilerParams(vmem_limit_bytes=8 * 1024 * 1024),
    )(final, rows, spread)
    return result[None]


def solution(mesh):
    in_specs = (
        P("segment", None, ("expert", "dp"), None),
        P(None, None, ("expert", "dp"), None),
        P("segment", None, None, ("expert", "dp"), None),
        P("segment", None, None, None, ("expert", "dp"), None),
        P("segment", None, None, None, ("expert", "dp"), None),
        P("segment", "expert", None, "dp"),
        P("segment", "expert", None, "dp"),
        P("segment", "expert", "dp", None),
        P("segment", None, None),
    )
    out_specs = P("segment", None, ("expert", "dp"), None)
    sizes = (mesh.shape["segment"], mesh.shape["expert"], mesh.shape["dp"])
    body = functools.partial(local, sizes)
    return jax.shard_map(body, mesh=mesh, in_specs=in_specs, out_specs=out_specs, check_vma=False)
```

```python
import functools
import jax
import jax.numpy as jnp
from jax import lax
from jax.experimental import pallas as pl
from jax.experimental.pallas import tpu as pltpu
from jax.sharding import PartitionSpec as P

CAP = 8
EPSILON = 1e-06
LAST = (((1,), (1,)), ((), ()))
MESH = pl.DeviceIdType.MESH
BF = jnp.bfloat16
F32 = jnp.float32
OUT = ("k0a", "f00", "d0b", "k1a", "k0b", "f01", "k1b", "d0a", "f10", "d1b", "f11", "d1a")
BACK = ("k0a", "f00", "k1a", "d0b", "f01", "d0a", "f10", "d1b", "f11", "d1a")
VALS = ("fx1", "fx2", "k0a", "k0b", "k1a", "k1b", "d0a", "d0b", "d1a", "d1b")
INVS = ("0a", "0b", "1a", "1b")
PRES = ("k0a", "k0b", "k1a", "k1b")
STREAMS = range(2)


def mm(a, b):
    return jnp.dot(a, b, preferred_element_type=F32)


def mm_t(a, b):
    return lax.dot_general(a, b, LAST, preferred_element_type=F32)


def mix(picks, rows):
    high = rows.astype(BF).astype(F32)
    rest = rows - high
    mid = rest.astype(BF).astype(F32)
    parts = jnp.concatenate([high, mid, rest - mid])
    return mm(picks.astype(BF), parts.astype(BF))


def unit_norm(rows, gain):
    inv = lax.rsqrt(jnp.mean(rows * rows, axis=-1, keepdims=True) + EPSILON)
    return rows * inv * gain, inv


def back_norm(rows, inv, gain, grad):
    weighted = gain * grad
    total = jnp.sum(weighted * rows, axis=-1, keepdims=True)
    return inv * weighted - rows * (inv * inv * inv) * total / rows.shape[-1]


def quotient(a, b):
    return a // b if isinstance(a, int) else lax.div(a, b)


def remainder(a, b):
    return a % b if isinstance(a, int) else lax.rem(a, b)


def kernel(sizes, state_in, entering, saved_in, ids_in, gates_in, wg_in, wu_in, wd_in, gains_in,
           final, rows_out, spread_out,
           outs, ins, bouts, bins, base, ids, gates, gains, state, saved, patch_out, patch_in, held_out, held_in,
           sel, gate_col, overlaps, moves, fresh_base, vals, invs, pre, early, hold, wg, wu, wd, wgn, wun, wdn,
           send_sem, recv_sem, back_sem, relay_send, relay_recv, weight_sem,
           pair_send, pair_recv, input_sem, small_sem):
    ns, ne, nd = sizes
    nh = nd // 2
    group = ne * nh
    ec = ne // 2
    width = ec * CAP
    tokens, model = state_in.shape[1], state_in.shape[2]
    hidden = wg_in.shape[0]
    hm = model // 2
    gr = group * CAP
    seg, ex, dp = lax.axis_index("segment"), lax.axis_index("expert"), lax.axis_index("dp")
    half, side = lax.div(dp, 2), lax.rem(dp, 2)
    me = ex * nh + half

    saved_copies = [pltpu.make_async_copy(saved_in.at[s], saved.at[s], input_sem.at[s]) for s in range(2)]
    state_copies = [
        pltpu.make_async_copy(state_in.at[pl.ds(2 * i, 2)], state.at[pl.ds(2 * i, 2)], input_sem.at[2 + i])
        for i in range(2)
    ]
    small_copies = [
        pltpu.make_async_copy(source, dest, small_sem.at[i])
        for i, (source, dest) in enumerate(((ids_in, ids), (gates_in, gates), (gains_in, gains)))
    ]
    for copy in (*small_copies, saved_copies[0]):
        copy.start()

    barrier = pltpu.get_barrier_semaphore()

    def each_peer(body):
        if group <= 8:
            for k in reversed(range(1, group)):
                body(k)
        else:
            pl.loop(1, group)(body)

    def peer(k):
        te = lax.rem(ex + quotient(k, nh), ne)
        th = lax.rem(half + remainder(k, nh), nh)
        return te, th, (seg, te, th * 2 + 1 - side)

    partner = (seg, ex, half * 2 + 1 - side)
    has_up, has_down = seg < ns - 1, seg > 0

    def greet(k):
        pl.semaphore_signal(barrier, inc=1, device_id=peer(k)[2], device_id_type=MESH)

    each_peer(greet)
    pl.semaphore_signal(barrier, inc=1, device_id=partner, device_id_type=MESH)

    @pl.when(has_up)
    def _():
        pl.semaphore_signal(barrier, inc=1, device_id=(seg + 1, ex, dp), device_id_type=MESH)

    @pl.when(has_down)
    def _():
        pl.semaphore_signal(barrier, inc=1, device_id=(seg - 1, ex, dp), device_id_type=MESH)

    weights = ((wg_in, wg), (wu_in, wu), (wd_in, wd))
    weight_copies = [
        pltpu.make_async_copy(source, dest.at[pl.ds(0, hidden)], weight_sem.at[i])
        for i, (source, dest) in enumerate(weights)
    ]
    pieces = [(source, dest.at[pl.ds(hidden, hidden)]) for source, dest in weights[:2]] + [
        (wd_in.at[:, pl.ds(hf * hm, hm)], wd.at[pl.ds(hidden, hidden), pl.ds(hf * hm, hm)]) for hf in range(2)
    ]
    pair_copies = [
        pltpu.make_async_remote_copy(
            src_ref=source, dst_ref=dest, send_sem=pair_send.at[i],
            recv_sem=pair_recv.at[i], device_id=partner, device_id_type=MESH,
        )
        for i, (source, dest) in enumerate(pieces)
    ]
    for copy in (state_copies[0], *weight_copies, saved_copies[1], state_copies[1]):
        copy.start()

    units = state_in.shape[0]
    lane = lax.broadcasted_iota(jnp.int32, (tokens, tokens), 1)
    row = lax.broadcasted_iota(jnp.int32, (tokens, tokens), 0)
    before = (row < lane).astype(F32).astype(BF)
    eye = (row == lane).astype(F32)
    slot_row = lax.broadcasted_iota(jnp.int32, (CAP, tokens), 0).astype(F32)
    su = 2 * units
    topk = ids.shape[0] // (2 * su)

    def tab(slot, unit, sub):
        return sub * su + slot * units + unit

    small_copies[0].wait()
    small_copies[1].wait()
    for e in range(ec):
        routed, weight = [], []
        for j in range(2):
            count, total = jnp.zeros((su, tokens), F32), jnp.zeros((su, tokens), F32)
            for k in range(topk):
                rows = pl.ds(k * 2 + j, su, stride=2 * topk)
                match = ids[rows, :] == e
                count = count + match.astype(F32)
                total = total + jnp.where(match, gates[rows, :], 0.0)
            routed.append(count)
            weight.append(total)
        routed = jnp.concatenate(routed)
        weight = jnp.concatenate(weight)
        earlier = mm(routed.astype(BF), before)
        for tb in range(2 * su):
            hit = (routed[tb:tb + 1] == 1.0) & (earlier[tb:tb + 1] == slot_row)
            one = jnp.where(hit, 1.0, 0.0)
            sel[tb, e * CAP:(e + 1) * CAP] = one
            gate_col[tb, e * CAP:(e + 1) * CAP] = jnp.broadcast_to(
                jnp.sum(one * weight[tb:tb + 1], axis=1, keepdims=True), (CAP, tokens)
            )

    def first_second(slot, unit):
        first = unit % 2
        return sel[tab(slot, unit, first)], sel[tab(slot, unit, 1 - first)]

    def last_picks(slot, unit):
        s1, s2 = first_second(slot, unit)
        if unit < 2:
            s1 = s1 * (1.0 - jnp.sum(s2, axis=0, keepdims=True))
        else:
            s2 = s2 * (1.0 - jnp.sum(s1, axis=0, keepdims=True))
        return jnp.concatenate([s1, s2])

    def both_picks(slot, unit):
        return jnp.concatenate(first_second(slot, unit))

    def pick(slot, unit, values):
        return mm(both_picks(slot, unit).astype(BF), values)

    def gate(slot, unit, second):
        sub = 1 - unit % 2 if second else unit % 2
        return gate_col[tab(slot, unit, sub)][:, 0:1]

    def gain(unit, second):
        sub = 1 - unit % 2 if second else unit % 2
        return gains[sub:sub + 1]

    def relay(unit, kind, source, dest):
        up = unit in (0, 3)
        goes, comes = (has_up, has_down) if up else (has_down, has_up)
        target = lax.rem(seg + (1 if up else ns - 1), ns)
        copy = pltpu.make_async_remote_copy(
            src_ref=source, dst_ref=dest, send_sem=relay_send.at[kind, 0 if up else 1],
            recv_sem=relay_recv.at[kind, unit], device_id=(target, ex, dp), device_id_type=MESH,
        )
        return goes, comes, copy

    def start_if(triple):
        @pl.when(triple[0])
        def _():
            triple[2].start()

    def arrive_if(triple):
        @pl.when(triple[1])
        def _():
            triple[2].wait_recv()

    bulk = [relay(u, 0, state_in.at[u], base.at[u]) for u in range(4)]
    enter = [pltpu.make_async_copy(entering.at[u], base.at[u], relay_recv.at[0, u]) for u in range(4)]
    patches = [[relay(u, 1 + i, patch_out.at[u, i], patch_in.at[u, i]) for i in range(2)] for u in range(4)]
    helds = [relay(u, 3, held_out.at[u], held_in.at[u]) for u in range(4)]

    def wait_bulk(u):
        arrive_if(bulk[u])

        @pl.when(jnp.logical_not(bulk[u][1]))
        def _():
            enter[u].wait()

    def out_copy(name, hf, k):
        i = OUT.index(name)
        te, th, device = peer(k)
        return pltpu.make_async_remote_copy(
            src_ref=outs.at[i, hf, te], dst_ref=ins.at[i, hf, me], send_sem=send_sem.at[0],
            recv_sem=recv_sem.at[i, hf], device_id=device, device_id_type=MESH,
        )

    def back_copy(name, hf, k):
        i = BACK.index(name)
        te, th, device = peer(k)
        return pltpu.make_async_remote_copy(
            src_ref=bouts.at[i, hf, te * nh + th], dst_ref=bins.at[i, hf, me], send_sem=send_sem.at[1 if i + 1 < len(BACK) else 2],
            recv_sem=back_sem.at[i], device_id=device, device_id_type=MESH,
        )

    def send_out(name):
        i = OUT.index(name)
        for hf in range(2):
            each_peer(lambda k, hf=hf: out_copy(name, hf, k).start())
        for hf in range(2):
            pltpu.make_async_copy(outs.at[i, hf, ex], ins.at[i, hf, me], recv_sem.at[i, hf]).start()

    def send_back(name, hf):
        i = BACK.index(name)
        each_peer(lambda k: back_copy(name, hf, k).start())
        pltpu.make_async_copy(bouts.at[i, hf, me], bins.at[i, hf, me], back_sem.at[i]).start()

    def take_out(name, hf):
        i = OUT.index(name)
        pltpu.make_async_copy(ins.at[i, hf], ins.at[i, hf], recv_sem.at[i, hf]).wait()

    def take_back(name):
        i = BACK.index(name)
        pltpu.make_async_copy(bins.at[i], bins.at[i], back_sem.at[i]).wait()

    def put(name, unit, second, rows):
        j = 1 - unit % 2 if second else unit % 2
        for e in range(ec):
            for hf in range(2):
                outs[OUT.index(name), hf, j * ec + e] = (
                    rows[e * CAP:(e + 1) * CAP, hf * hm:(hf + 1) * hm].astype(BF)
                )

    def got(name, unit, second):
        j = 1 - unit % 2 if second else unit % 2
        i = BACK.index(name)
        parts = []
        for e in range(ec):
            first = (j * ec + e) * nh
            halves = []
            for hf in range(2):
                total = bins[i, hf, first].astype(F32)
                for q in range(1, nh):
                    total = total + bins[i, hf, first + q].astype(F32)
                halves.append(total)
            parts.append(jnp.concatenate(halves, axis=1))
        return parts[0] if ec == 1 else jnp.concatenate(parts)

    def rows_of(hf, *names):
        parts = [ins[OUT.index(name), hf].astype(F32).reshape(gr, hm) for name in names]
        return (parts[0] if len(parts) == 1 else jnp.concatenate(parts)).astype(BF)

    def give(name, hf, rows):
        bouts[BACK.index(name), hf] = rows.reshape(group, CAP, hm).astype(BF)

    def cut(weight, hf):
        return weight[:, hf * hm:(hf + 1) * hm]

    def turn(source, dest):
        for c in range(0, model, 256):
            dest[c:c + 256] = source[:, c:c + 256].T

    def product(rows, weight, hf):
        if weight.shape[0] == model:
            return mm(rows, weight[hf * hm:(hf + 1) * hm])
        return mm_t(rows, cut(weight, hf))

    def inward(weights, *names, ready=None):
        sums = [None] * len(weights)
        for hf in range(2):
            for name in names:
                take_out(name, hf)
            if ready is not None:
                continue
            rows = rows_of(hf, *names)
            for i, weight in enumerate(weights):
                part = product(rows, weight, hf)
                if hf == 0:
                    hold[i, :len(names) * gr] = part
                else:
                    sums[i] = part + hold[i, :len(names) * gr]
        if ready is not None:
            for i, weight in enumerate(weights):
                ready(i)
                sums[i] = product(rows_of(0, *names), weight, 0) + product(rows_of(1, *names), weight, 1)
        return sums

    def activate(gp, up):
        return (gp * jax.nn.sigmoid(gp) * up).astype(BF)

    def outward(names, pairs, ready=None):
        for hf in range(2):
            if ready is not None:
                ready(2 + hf)
            total = mm(pairs[0][0], cut(pairs[0][1], hf))
            for a, weight in pairs[1:]:
                total = total + mm(a, cut(weight, hf))
            for n, name in enumerate(names):
                give(name, hf, total[n * gr:(n + 1) * gr])
                send_back(name, hf)

    def backward(name, act, gp, up):
        sig = jax.nn.sigmoid(gp)
        grad_gate = (act * up * sig * (1.0 + gp * (1.0 - sig))).astype(BF)
        grad_up = (act * gp * sig).astype(BF)
        outward((name,), ((grad_gate, wg), (grad_up, wu)))

    def at(name, st):
        return VALS.index(name) * 2 + st

    def inv_at(slot, which, st):
        return INVS.index(f"{slot}{which}") * 2 + st

    def keep_inv(slot, which, st, inv):
        invs[inv_at(slot, which, st)] = jnp.broadcast_to(inv, (width, tokens))

    def held_inv(slot, which, st):
        return invs[inv_at(slot, which, st)][:, 0:1]

    def pre_at(name):
        i = PRES.index(name) * 2
        return pre[i], pre[i + 1]

    def keep_pre(name, values):
        i = PRES.index(name) * 2
        pre[i], pre[i + 1] = values

    def crossing(slot, unit, transposed):
        s1, s2 = first_second(slot, unit)
        if transposed:
            s1, s2 = s2, s1
        return mm_t(s2.astype(BF), jnp.concatenate([s1, s1, s1]).astype(BF))

    def over_at(slot, unit, transposed):
        return slot * 6 + unit + (2 if transposed else 0)

    def start_kept(slot):
        name = f"k{slot}a"
        saved_copies[slot].wait()
        for st in STREAMS:
            b = 2 + st
            both = pick(slot, b, saved[slot, st])
            vals[at(f"k{slot}a", st)], vals[at(f"k{slot}b", st)] = both[:width], both[width:]
            rows, inv = unit_norm(both[:width], gain(b, False))
            put(name, b, False, rows)
            keep_inv(slot, "a", st, inv)

    def middle_kept(slot):
        take_back(f"k{slot}a")
        for st in STREAMS:
            b = 2 + st
            add = gate(slot, b, False) * got(f"k{slot}a", b, False)
            middle = vals[at(f"k{slot}b", st)] + mix(overlaps[over_at(slot, b, False)], add)
            vals[at(f"k{slot}b", st)] = middle
            rows, inv = unit_norm(middle, gain(b, True))
            put(f"k{slot}b", b, True, rows)
            keep_inv(slot, "b", st, inv)
        send_out(f"k{slot}b")

    def forward_start(slot, st, first, second):
        vals[at("fx1", st)], vals[at("fx2", st)] = first, second
        put(f"f{slot}0", st, False, unit_norm(first, gain(st, False))[0])

    def send_patch(u, part, rows):
        patch_out[u, part] = rows.astype(BF)
        start_if(patches[u][part])

    def forward_middle(slot):
        take_back(f"f{slot}0")
        for st in STREAMS:
            add = gate(slot, st, False) * got(f"f{slot}0", st, False)
            vals[at("fx1", st)] = vals[at("fx1", st)] + add
            middle = vals[at("fx2", st)] + mix(overlaps[over_at(slot, st, False)], add)
            vals[at("fx2", st)] = middle
            put(f"f{slot}1", st, True, unit_norm(middle, gain(st, True))[0])
        send_out(f"f{slot}1")

    def forward_end(slot, st):
        return vals[at("fx2", st)] + gate(slot, st, True) * got(f"f{slot}1", st, True)

    def backward_start(slot, st, first, second):
        vals[at(f"d{slot}a", st)], vals[at(f"d{slot}b", st)] = first, second
        put(f"d{slot}b", 2 + st, True, gate(slot, 2 + st, True) * second)

    def backward_middle(slot):
        take_back(f"d{slot}b")
        for st in STREAMS:
            b = 2 + st
            step = back_norm(
                vals[at(f"k{slot}b", st)], held_inv(slot, "b", st), gain(b, True), got(f"d{slot}b", b, True)
            )
            inner = vals[at(f"d{slot}a", st)] + mix(overlaps[over_at(slot, b, True)], step)
            put(f"d{slot}a", b, False, gate(slot, b, False) * inner)
            vals[at(f"d{slot}b", st)] = vals[at(f"d{slot}b", st)] + step
            vals[at(f"d{slot}a", st)] = inner
        send_out(f"d{slot}a")

    def backward_end(slot, st):
        b = 2 + st
        return vals[at(f"d{slot}a", st)] + back_norm(
            vals[at(f"k{slot}a", st)], held_inv(slot, "a", st), gain(b, False), got(f"d{slot}a", b, False)
        )

    def expert_forward(name, weights):
        gp, up = inward(weights, name)
        outward((name,), ((activate(gp, up), wd),))

    def expert_backward(name, pres):
        act, = inward((wdn,), name)
        backward(name, act, *pre_at(pres))

    def ready_unit(u):
        last = 1 if u < 2 else 0
        wait_bulk(u)
        arrive_if(helds[u])
        arrive_if(patches[u][1 - last])
        held = held_in[u].astype(F32)
        both = both_picks(1, u)
        keep = 1.0 - jnp.sum(held, axis=0, keepdims=True)
        parts = [mm_t(both.astype(BF), held[i * width:(i + 1) * width].astype(BF)) for i in range(2)]
        moves[u] = parts[last]
        fresh_base[u] = mm((both * keep).astype(BF), base[u]) + mm(parts[1 - last].astype(BF), patch_in[u, 1 - last])

    def pick_new(u):
        last = 1 if u < 2 else 0
        arrive_if(patches[u][last])
        return fresh_base[u] + mm(moves[u].astype(BF), patch_in[u, last])

    def settle(u, parts):
        new_sel = last_picks(1, u)
        fresh = 1.0 - jnp.sum(new_sel, axis=0, keepdims=True)
        old_sel = held_in[u].astype(F32) * fresh
        kept = eye * (fresh - jnp.sum(old_sel, axis=0, keepdims=True))
        picks = [old_sel] + [new_sel[i * width:(i + 1) * width] for i, _ in parts]
        rows = [patch_in[u, i].astype(F32) for i in range(2)] + [value for _, value in parts]
        spread = mm_t(eye.astype(BF), jnp.concatenate(picks).astype(BF))
        final[u] = (
            mm(kept.astype(BF), base[u]) + mm(spread.astype(BF), jnp.concatenate(rows).astype(BF))
        ).astype(BF)
        if u >= 2:
            spread_out[u - 2] = mm_t(eye.astype(BF), new_sel[:width].astype(BF)).astype(BF)

    def drain(buffer, i):
        sent = buffer.at[:, :, pl.ds(0, group - 1)]
        pltpu.make_async_copy(sent, sent, send_sem.at[i]).wait()

    neighbours = jnp.where(has_up, 1, 0) + jnp.where(has_down, 1, 0)
    pl.semaphore_wait(barrier, group + neighbours)
    for copy in pair_copies:
        copy.start()
    small_copies[2].wait()
    start_kept(0)
    send_out("k0a")
    state_copies[0].wait()
    for st in STREAMS:
        both = pick(0, st, state[st])
        forward_start(0, st, both[:width], both[width:])
    send_out("f00")
    start_kept(1)
    send_out("k1a")
    state_copies[1].wait()
    for st in STREAMS:
        both = pick(0, 2 + st, state[2 + st])
        backward_start(0, st, both[:width], both[width:])
    send_out("d0b")

    for u in range(4):
        held_out[u] = last_picks(0, u).astype(BF)
    for u in range(4):
        start_if(helds[u])

        @pl.when(jnp.logical_not(helds[u][1]))
        def _(u=u):
            patch_in[u] = jnp.zeros(patch_in.shape[1:], BF)
            held_in[u] = jnp.zeros(held_in.shape[1:], BF)
    for u in range(4):
        start_if(bulk[u])

        @pl.when(jnp.logical_not(bulk[u][1]))
        def _(u=u):
            enter[u].start()
    for slot in range(2):
        for u in range(4):
            overlaps[over_at(slot, u, False)] = crossing(slot, u, False)
            if u >= 2:
                overlaps[over_at(slot, u, True)] = crossing(slot, u, True)

    def wait_weight(i):
        if i < 3:
            weight_copies[i].wait()
        pair_copies[i].wait_recv()

    gp, up = inward((wg, wu), "k0a", ready=wait_weight)
    keep_pre("k0a", (gp, up))
    outward(("k0a",), ((activate(gp, up), wd),), wait_weight)
    expert_forward("f00", (wg, wu))
    middle_kept(0)
    turn(wd, wdn)
    early[...], = inward((wdn,), "d0b")
    turn(wg, wgn)
    turn(wu, wun)
    gp, up = inward((wgn, wun), "k0b")
    backward("d0b", early[...], gp, up)
    forward_middle(0)
    for st in STREAMS:
        send_patch(st, 0, vals[at("fx1", st)])
    backward_middle(0)
    for st in STREAMS:
        send_patch(2 + st, 1, vals[at("d0b", st)])
    gp, up = inward((wgn, wun), "f01", "k1a")
    outward(("f01", "k1a"), ((activate(gp, up), wd),))
    keep_pre("k1a", (gp[gr:], up[gr:]))
    expert_backward("d0a", "k0a")
    take_back("f01")
    for st in STREAMS:
        send_patch(st, 1, forward_end(0, st))
    for st in STREAMS:
        ready_unit(2 + st)
    middle_kept(1)
    take_back("d0a")
    for st in STREAMS:
        send_patch(2 + st, 0, backward_end(0, st))
    for st in STREAMS:
        ready_unit(st)
    for st in STREAMS:
        both = pick_new(st)
        forward_start(1, st, both[:width], both[width:])
    send_out("f10")
    for st in STREAMS:
        both = pick_new(2 + st)
        backward_start(1, st, both[:width], both[width:])
    send_out("d1b")
    gp, up = inward((wgn, wun), "f10", "k1b")
    outward(("f10",), ((activate(gp[:gr], up[:gr]), wd),))
    keep_pre("k1b", (gp[gr:], up[gr:]))
    expert_backward("d1b", "k1b")
    forward_middle(1)
    backward_middle(1)
    expert_forward("f11", (wgn, wun))
    expert_backward("d1a", "k1a")
    for st in STREAMS:
        settle(2 + st, [(1, vals[at("d1b", st)])])
    take_back("f11")
    for st in STREAMS:
        settle(st, [(0, vals[at("fx1", st)]), (1, forward_end(1, st))])
    drain(ins, 0)
    drain(bins.at[pl.ds(0, len(BACK) - 1)], 1)
    for copy in pair_copies:
        copy.wait_send()
    for goes, way in ((has_up, 0), (has_down, 1)):
        @pl.when(goes)
        def _(way=way):
            pairs = (base.at[pl.ds(0, 2)], patch_in.at[0], patch_in.at[0], held_in.at[pl.ds(0, 2)])
            for kind, sent in enumerate(pairs):
                pltpu.make_async_copy(sent, sent, relay_send.at[kind, way]).wait()
    take_back("d1a")
    for st in STREAMS:
        rows_out[st] = backward_end(1, st).astype(BF)
    drain(bins.at[pl.ds(0, 1)], 2)


def merge(final, rows, spread, out, merged, out_sem):
    units = final.shape[0]
    sources = [final.at[u] if u < 2 else merged.at[u - 2] for u in range(units)]
    copies = [pltpu.make_async_copy(sources[u], out.at[u], out_sem.at[u]) for u in range(units)]
    for u in range(units):
        if u >= 2:
            merged[u - 2] = (final[u].astype(F32) + mm(spread[u - 2], rows[u - 2])).astype(BF)
        copies[u].start()
    for copy in copies:
        copy.wait()


def stay(value):
    return pltpu.with_memory_space_constraint(value, pltpu.HBM)


def local(sizes, state_in, entering, saved, route_ids, gate_vals, w_gate, w_up, w_down, gains):
    ns, ne, nd = sizes
    group, width = ne * nd // 2, ne // 2 * CAP
    units, tokens, model = state_in.shape[1:]
    hidden = w_gate.shape[-1]
    tables = route_ids.shape[1] * route_ids.shape[2] * route_ids.shape[3]
    topk = route_ids.shape[-1]
    turn = (0, 1, 2, 5, 3, 4)
    ids = jnp.transpose(route_ids, turn).reshape(tables * topk, tokens)
    gates = jnp.transpose(gate_vals, turn).reshape(tables * topk, tokens)
    vmem = pl.BlockSpec(memory_space=pltpu.VMEM)
    anywhere = pl.BlockSpec(memory_space=pl.ANY)
    dma = pltpu.SemaphoreType.DMA
    scratch = [
        pltpu.VMEM((len(OUT), 2, ne, CAP, model // 2), BF),
        pltpu.VMEM((len(OUT), 2, group, CAP, model // 2), BF),
        pltpu.VMEM((len(BACK), 2, group, CAP, model // 2), BF),
        pltpu.VMEM((len(BACK), 2, group, CAP, model // 2), BF),
        pltpu.VMEM((units, tokens, model), BF),
        pltpu.VMEM(ids.shape, jnp.int32),
        pltpu.VMEM(gates.shape, F32),
        pltpu.VMEM(gains.shape[1:], F32),
        pltpu.VMEM((units, tokens, model), BF),
        pltpu.VMEM(saved.shape[1:], BF),
        pltpu.VMEM((units, 2, width, model), BF),
        pltpu.VMEM((units, 2, width, model), BF),
        pltpu.VMEM((units, 2 * width, tokens), BF),
        pltpu.VMEM((units, 2 * width, tokens), BF),
        pltpu.VMEM((tables, width, tokens), F32),
        pltpu.VMEM((tables, width, tokens), F32),
        pltpu.VMEM((12, width, 3 * width), F32),
        pltpu.VMEM((units, 2 * width, width), F32),
        pltpu.VMEM((units, 2 * width, model), F32),
        pltpu.VMEM((2 * len(VALS), width, model), F32),
        pltpu.VMEM((2 * len(INVS), width, tokens), F32),
        pltpu.VMEM((2 * len(PRES), group * CAP, 2 * hidden), F32),
        pltpu.VMEM((group * CAP, 2 * hidden), F32),
        pltpu.VMEM((2, 2 * group * CAP, 2 * hidden), F32),
        pltpu.VMEM((2 * hidden, model), BF),
        pltpu.VMEM((2 * hidden, model), BF),
        pltpu.VMEM((2 * hidden, model), BF),
        pltpu.VMEM((model, 2 * hidden), BF),
        pltpu.VMEM((model, 2 * hidden), BF),
        pltpu.VMEM((model, 2 * hidden), BF),
        dma((3,)), dma((len(OUT), 2)), dma((len(BACK),)),
        dma((4, 2)), dma((4, units)), dma((3,)),
        dma((4,)), dma((4,)), dma((4,)), dma((3,)),
    ]
    final, rows, spread = pl.pallas_call(
        functools.partial(kernel, sizes),
        out_shape=(
            jax.ShapeDtypeStruct((units, tokens, model), BF),
            jax.ShapeDtypeStruct((2, width, model), BF),
            jax.ShapeDtypeStruct((2, tokens, width), BF),
        ),
        in_specs=[anywhere] * 9,
        out_specs=(vmem, vmem, vmem),
        scratch_shapes=scratch,
        compiler_params=pltpu.CompilerParams(
            collective_id=0, has_side_effects=True, vmem_limit_bytes=46137344 if ne <= 4 else 67043328
        ),
    )(*map(stay, (
        state_in[0], entering[0], saved[0], ids, gates, jnp.swapaxes(w_gate[0, 0], 0, 1),
        jnp.swapaxes(w_up[0, 0], 0, 1), w_down[0, 0], gains[0],
    )))
    result = pl.pallas_call(
        merge,
        out_shape=jax.ShapeDtypeStruct((units, tokens, model), BF),
        in_specs=[vmem] * 3,
        out_specs=pl.BlockSpec(memory_space=pltpu.HBM),
        scratch_shapes=[
            pltpu.VMEM((units - 2, tokens, model), BF), dma((units,)),
        ],
        compiler_params=pltpu.CompilerParams(vmem_limit_bytes=8 * 1024 * 1024),
    )(final, rows, spread)
    return result[None]


def solution(mesh):
    in_specs = (
        P("segment", None, ("expert", "dp"), None),
        P(None, None, ("expert", "dp"), None),
        P("segment", None, None, ("expert", "dp"), None),
        P("segment", None, None, None, ("expert", "dp"), None),
        P("segment", None, None, None, ("expert", "dp"), None),
        P("segment", "expert", None, "dp"),
        P("segment", "expert", None, "dp"),
        P("segment", "expert", "dp", None),
        P("segment", None, None),
    )
    out_specs = P("segment", None, ("expert", "dp"), None)
    sizes = (mesh.shape["segment"], mesh.shape["expert"], mesh.shape["dp"])
    body = functools.partial(local, sizes)
    return jax.shard_map(body, mesh=mesh, in_specs=in_specs, out_specs=out_specs, check_vma=False)
```

```python
import functools
import jax
import jax.numpy as jnp
from jax import lax
from jax.experimental import pallas as pl
from jax.experimental.pallas import tpu as pltpu
from jax.sharding import PartitionSpec as P

CAP = 8
EPSILON = 1e-06
LAST = (((1,), (1,)), ((), ()))
MESH = pl.DeviceIdType.MESH
BF = jnp.bfloat16
F32 = jnp.float32
OUT = ("k0a", "f00", "d0b", "k1a", "k0b", "f01", "k1b", "d0a", "f10", "d1b", "f11", "d1a")
BACK = ("k0a", "f00", "k1a", "d0b", "f01", "d0a", "f10", "d1b", "f11", "d1a")
VALS = ("fx1", "fx2", "k0a", "k0b", "k1a", "k1b", "d0a", "d0b", "d1a", "d1b")
INVS = ("0a", "0b", "1a", "1b")
PRES = ("k0a", "k0b", "k1a", "k1b")
STREAMS = range(2)
CUTS_OUT = 2
CUTS_BACK = 2


def mm(a, b):
    return jnp.dot(a, b, preferred_element_type=F32)


def mm_t(a, b):
    return lax.dot_general(a, b, LAST, preferred_element_type=F32)


def mix(picks, rows):
    high = rows.astype(BF).astype(F32)
    rest = rows - high
    mid = rest.astype(BF).astype(F32)
    parts = jnp.concatenate([high, mid, rest - mid])
    return mm(picks.astype(BF), parts.astype(BF))


def unit_norm(rows, gain):
    inv = lax.rsqrt(jnp.mean(rows * rows, axis=-1, keepdims=True) + EPSILON)
    return rows * inv * gain, inv


def back_norm(rows, inv, gain, grad):
    weighted = gain * grad
    total = jnp.sum(weighted * rows, axis=-1, keepdims=True)
    return inv * weighted - rows * (inv * inv * inv) * total / rows.shape[-1]


def quotient(a, b):
    return a // b if isinstance(a, int) else lax.div(a, b)


def remainder(a, b):
    return a % b if isinstance(a, int) else lax.rem(a, b)


def kernel(sizes, state_in, entering, saved_in, ids_in, gates_in, wg_in, wu_in, wd_in, gains_in,
           final, rows_out, spread_out,
           outs, ins, bouts, bins, base, ids, gates, gains, state, saved, patch_out, patch_in, held_out, held_in,
           sel, gate_col, overlaps, moves, fresh_base, vals, invs, pre, early, hold, wg, wu, wd, wgn, wun, wdn,
           send_sem, recv_sem, back_sem, relay_send, relay_recv, weight_sem,
           pair_send, pair_recv, input_sem, small_sem):
    ns, ne, nd = sizes
    nh = nd // 2
    group = ne * nh
    ec = ne // 2
    width = ec * CAP
    tokens, model = state_in.shape[1], state_in.shape[2]
    hidden = wg_in.shape[0]
    ho, hb = model // CUTS_OUT, model // CUTS_BACK
    gr = group * CAP
    seg, ex, dp = lax.axis_index("segment"), lax.axis_index("expert"), lax.axis_index("dp")
    half, side = lax.div(dp, 2), lax.rem(dp, 2)
    me = ex * nh + half

    saved_copies = [pltpu.make_async_copy(saved_in.at[s], saved.at[s], input_sem.at[s]) for s in range(2)]
    state_copies = [
        pltpu.make_async_copy(state_in.at[pl.ds(2 * i, 2)], state.at[pl.ds(2 * i, 2)], input_sem.at[2 + i])
        for i in range(2)
    ]
    small_copies = [
        pltpu.make_async_copy(source, dest, small_sem.at[i])
        for i, (source, dest) in enumerate(((ids_in, ids), (gates_in, gates), (gains_in, gains)))
    ]
    for copy in (*small_copies, saved_copies[0]):
        copy.start()

    barrier = pltpu.get_barrier_semaphore()

    def each_peer(body):
        if group <= 8:
            for k in reversed(range(1, group)):
                body(k)
        else:
            pl.loop(1, group)(body)

    def peer(k):
        te = lax.rem(ex + quotient(k, nh), ne)
        th = lax.rem(half + remainder(k, nh), nh)
        return te, th, (seg, te, th * 2 + 1 - side)

    partner = (seg, ex, half * 2 + 1 - side)
    has_up, has_down = seg < ns - 1, seg > 0

    def greet(k):
        pl.semaphore_signal(barrier, inc=1, device_id=peer(k)[2], device_id_type=MESH)

    each_peer(greet)
    pl.semaphore_signal(barrier, inc=1, device_id=partner, device_id_type=MESH)

    @pl.when(has_up)
    def _():
        pl.semaphore_signal(barrier, inc=1, device_id=(seg + 1, ex, dp), device_id_type=MESH)

    @pl.when(has_down)
    def _():
        pl.semaphore_signal(barrier, inc=1, device_id=(seg - 1, ex, dp), device_id_type=MESH)

    weights = ((wg_in, wg), (wu_in, wu), (wd_in, wd))
    weight_copies = [
        pltpu.make_async_copy(source, dest.at[pl.ds(0, hidden)], weight_sem.at[i])
        for i, (source, dest) in enumerate(weights)
    ]
    pieces = [(source, dest.at[pl.ds(hidden, hidden)]) for source, dest in weights[:2]] + [
        (wd_in.at[:, pl.ds(hf * hb, hb)], wd.at[pl.ds(hidden, hidden), pl.ds(hf * hb, hb)]) for hf in range(CUTS_BACK)
    ]
    pair_copies = [
        pltpu.make_async_remote_copy(
            src_ref=source, dst_ref=dest, send_sem=pair_send.at[i],
            recv_sem=pair_recv.at[i], device_id=partner, device_id_type=MESH,
        )
        for i, (source, dest) in enumerate(pieces)
    ]
    for copy in (state_copies[0], *weight_copies, saved_copies[1], state_copies[1]):
        copy.start()

    neighbours = jnp.where(has_up, 1, 0) + jnp.where(has_down, 1, 0)
    pl.semaphore_wait(barrier, group + neighbours)
    for copy in pair_copies:
        copy.start()

    def relay(unit, kind, source, dest):
        up = unit in (0, 3)
        goes, comes = (has_up, has_down) if up else (has_down, has_up)
        target = lax.rem(seg + (1 if up else ns - 1), ns)
        copy = pltpu.make_async_remote_copy(
            src_ref=source, dst_ref=dest, send_sem=relay_send.at[kind, 0 if up else 1],
            recv_sem=relay_recv.at[kind, unit], device_id=(target, ex, dp), device_id_type=MESH,
        )
        return goes, comes, copy

    def start_if(triple):
        @pl.when(triple[0])
        def _():
            triple[2].start()

    def arrive_if(triple):
        @pl.when(triple[1])
        def _():
            triple[2].wait_recv()

    bulk = [relay(u, 0, state_in.at[u], base.at[u]) for u in range(4)]
    enter = [pltpu.make_async_copy(entering.at[u], base.at[u], relay_recv.at[0, u]) for u in range(4)]
    for u in range(4):
        start_if(bulk[u])

        @pl.when(jnp.logical_not(bulk[u][1]))
        def _(u=u):
            enter[u].start()

    units = state_in.shape[0]
    lane = lax.broadcasted_iota(jnp.int32, (tokens, tokens), 1)
    row = lax.broadcasted_iota(jnp.int32, (tokens, tokens), 0)
    before = (row < lane).astype(F32).astype(BF)
    eye = (row == lane).astype(F32)
    slot_row = lax.broadcasted_iota(jnp.int32, (CAP, tokens), 0).astype(F32)
    su = 2 * units
    topk = ids.shape[0] // (2 * su)

    def tab(slot, unit, sub):
        return sub * su + slot * units + unit

    small_copies[0].wait()
    small_copies[1].wait()
    for e in range(ec):
        routed, weight = [], []
        for j in range(2):
            count, total = jnp.zeros((su, tokens), F32), jnp.zeros((su, tokens), F32)
            for k in range(topk):
                rows = pl.ds(k * 2 + j, su, stride=2 * topk)
                match = ids[rows, :] == e
                count = count + match.astype(F32)
                total = total + jnp.where(match, gates[rows, :], 0.0)
            routed.append(count)
            weight.append(total)
        routed = jnp.concatenate(routed)
        weight = jnp.concatenate(weight)
        earlier = mm(routed.astype(BF), before)
        for tb in range(2 * su):
            hit = (routed[tb:tb + 1] == 1.0) & (earlier[tb:tb + 1] == slot_row)
            one = jnp.where(hit, 1.0, 0.0)
            sel[tb, e * CAP:(e + 1) * CAP] = one
            gate_col[tb, e * CAP:(e + 1) * CAP] = jnp.broadcast_to(
                jnp.sum(one * weight[tb:tb + 1], axis=1, keepdims=True), (CAP, tokens)
            )

    def first_second(slot, unit):
        first = unit % 2
        return sel[tab(slot, unit, first)], sel[tab(slot, unit, 1 - first)]

    def last_picks(slot, unit):
        s1, s2 = first_second(slot, unit)
        if unit < 2:
            s1 = s1 * (1.0 - jnp.sum(s2, axis=0, keepdims=True))
        else:
            s2 = s2 * (1.0 - jnp.sum(s1, axis=0, keepdims=True))
        return jnp.concatenate([s1, s2])

    def both_picks(slot, unit):
        return jnp.concatenate(first_second(slot, unit))

    def pick(slot, unit, values):
        return mm(both_picks(slot, unit).astype(BF), values)

    def gate(slot, unit, second):
        sub = 1 - unit % 2 if second else unit % 2
        return gate_col[tab(slot, unit, sub)][:, 0:1]

    def gain(unit, second):
        sub = 1 - unit % 2 if second else unit % 2
        return gains[sub:sub + 1]

    patches = [[relay(u, 1 + i, patch_out.at[u, i], patch_in.at[u, i]) for i in range(2)] for u in range(4)]
    helds = [relay(u, 3, held_out.at[u], held_in.at[u]) for u in range(4)]

    def wait_bulk(u):
        arrive_if(bulk[u])

        @pl.when(jnp.logical_not(bulk[u][1]))
        def _():
            enter[u].wait()

    def out_copy(name, hf, k):
        i = OUT.index(name)
        te, th, device = peer(k)
        return pltpu.make_async_remote_copy(
            src_ref=outs.at[i, hf, te], dst_ref=ins.at[i, hf, me], send_sem=send_sem.at[0],
            recv_sem=recv_sem.at[i, hf], device_id=device, device_id_type=MESH,
        )

    def back_copy(name, hf, k):
        i = BACK.index(name)
        te, th, device = peer(k)
        return pltpu.make_async_remote_copy(
            src_ref=bouts.at[i, hf, te * nh + th], dst_ref=bins.at[i, hf, me], send_sem=send_sem.at[1 if i + 1 < len(BACK) else 2],
            recv_sem=back_sem.at[i], device_id=device, device_id_type=MESH,
        )

    def send_out(name):
        i = OUT.index(name)
        for hf in range(CUTS_OUT):
            each_peer(lambda k, hf=hf: out_copy(name, hf, k).start())
        for hf in range(CUTS_OUT):
            pltpu.make_async_copy(outs.at[i, hf, ex], ins.at[i, hf, me], recv_sem.at[i, hf]).start()

    def send_back(name, hf):
        i = BACK.index(name)
        each_peer(lambda k: back_copy(name, hf, k).start())
        pltpu.make_async_copy(bouts.at[i, hf, me], bins.at[i, hf, me], back_sem.at[i]).start()

    def take_out(name, hf):
        i = OUT.index(name)
        pltpu.make_async_copy(ins.at[i, hf], ins.at[i, hf], recv_sem.at[i, hf]).wait()

    def take_back(name):
        i = BACK.index(name)
        pltpu.make_async_copy(bins.at[i], bins.at[i], back_sem.at[i]).wait()

    def put(name, unit, second, rows):
        j = 1 - unit % 2 if second else unit % 2
        for e in range(ec):
            for hf in range(CUTS_OUT):
                outs[OUT.index(name), hf, j * ec + e] = (
                    rows[e * CAP:(e + 1) * CAP, hf * ho:(hf + 1) * ho].astype(BF)
                )

    def got(name, unit, second):
        j = 1 - unit % 2 if second else unit % 2
        i = BACK.index(name)
        parts = []
        for e in range(ec):
            first = (j * ec + e) * nh
            halves = []
            for hf in range(CUTS_BACK):
                total = bins[i, hf, first].astype(F32)
                for q in range(1, nh):
                    total = total + bins[i, hf, first + q].astype(F32)
                halves.append(total)
            parts.append(jnp.concatenate(halves, axis=1))
        return parts[0] if ec == 1 else jnp.concatenate(parts)

    def rows_of(hf, *names):
        parts = [ins[OUT.index(name), hf].astype(F32).reshape(gr, ho) for name in names]
        return (parts[0] if len(parts) == 1 else jnp.concatenate(parts)).astype(BF)

    def give(name, hf, rows):
        bouts[BACK.index(name), hf] = rows.reshape(group, CAP, hb).astype(BF)

    def cut(weight, hf):
        return weight[:, hf * hb:(hf + 1) * hb]

    def turn(source, dest):
        for c in range(0, model, 256):
            dest[c:c + 256] = source[:, c:c + 256].T

    def inward(weights, *names):
        sums = []
        for hf in range(CUTS_OUT):
            for name in names:
                take_out(name, hf)
            rows = rows_of(hf, *names)
            for i, weight in enumerate(weights):
                part = mm(rows, weight[hf * ho:(hf + 1) * ho])
                if hf > 0:
                    part = part + hold[i, :len(names) * gr]
                if hf + 1 < CUTS_OUT:
                    hold[i, :len(names) * gr] = part
                else:
                    sums.append(part)
        return sums

    def activate(gp, up):
        return (gp * jax.nn.sigmoid(gp) * up).astype(BF)

    def outward(names, pairs, ready=None):
        for hf in range(CUTS_BACK):
            if ready is not None:
                ready(2 + hf)
            total = mm(pairs[0][0], cut(pairs[0][1], hf))
            for a, weight in pairs[1:]:
                total = total + mm(a, cut(weight, hf))
            for n, name in enumerate(names):
                give(name, hf, total[n * gr:(n + 1) * gr])
                send_back(name, hf)

    def backward(name, act, gp, up):
        sig = jax.nn.sigmoid(gp)
        grad_gate = (act * up * sig * (1.0 + gp * (1.0 - sig))).astype(BF)
        grad_up = (act * gp * sig).astype(BF)
        outward((name,), ((grad_gate, wg), (grad_up, wu)))

    def at(name, st):
        return VALS.index(name) * 2 + st

    def inv_at(slot, which, st):
        return INVS.index(f"{slot}{which}") * 2 + st

    def keep_inv(slot, which, st, inv):
        invs[inv_at(slot, which, st)] = jnp.broadcast_to(inv, (width, tokens))

    def held_inv(slot, which, st):
        return invs[inv_at(slot, which, st)][:, 0:1]

    def pre_at(name):
        i = PRES.index(name) * 2
        return pre[i], pre[i + 1]

    def keep_pre(name, values):
        i = PRES.index(name) * 2
        pre[i], pre[i + 1] = values

    def crossing(slot, unit, transposed):
        s1, s2 = first_second(slot, unit)
        if transposed:
            s1, s2 = s2, s1
        return mm_t(s2.astype(BF), jnp.concatenate([s1, s1, s1]).astype(BF))

    def over_at(slot, unit, transposed):
        return slot * 6 + unit + (2 if transposed else 0)

    def start_kept(slot):
        name = f"k{slot}a"
        saved_copies[slot].wait()
        for st in STREAMS:
            b = 2 + st
            both = pick(slot, b, saved[slot, st])
            vals[at(f"k{slot}a", st)], vals[at(f"k{slot}b", st)] = both[:width], both[width:]
            rows, inv = unit_norm(both[:width], gain(b, False))
            put(name, b, False, rows)
            keep_inv(slot, "a", st, inv)

    def middle_kept(slot):
        take_back(f"k{slot}a")
        for st in STREAMS:
            b = 2 + st
            add = gate(slot, b, False) * got(f"k{slot}a", b, False)
            middle = vals[at(f"k{slot}b", st)] + mix(overlaps[over_at(slot, b, False)], add)
            vals[at(f"k{slot}b", st)] = middle
            rows, inv = unit_norm(middle, gain(b, True))
            put(f"k{slot}b", b, True, rows)
            keep_inv(slot, "b", st, inv)
        send_out(f"k{slot}b")

    def forward_start(slot, st, first, second):
        vals[at("fx1", st)], vals[at("fx2", st)] = first, second
        put(f"f{slot}0", st, False, unit_norm(first, gain(st, False))[0])

    def send_patch(u, part, rows):
        patch_out[u, part] = rows.astype(BF)
        start_if(patches[u][part])

    def forward_middle(slot):
        take_back(f"f{slot}0")
        for st in STREAMS:
            add = gate(slot, st, False) * got(f"f{slot}0", st, False)
            vals[at("fx1", st)] = vals[at("fx1", st)] + add
            middle = vals[at("fx2", st)] + mix(overlaps[over_at(slot, st, False)], add)
            vals[at("fx2", st)] = middle
            put(f"f{slot}1", st, True, unit_norm(middle, gain(st, True))[0])
        send_out(f"f{slot}1")

    def forward_end(slot, st):
        return vals[at("fx2", st)] + gate(slot, st, True) * got(f"f{slot}1", st, True)

    def backward_start(slot, st, first, second):
        vals[at(f"d{slot}a", st)], vals[at(f"d{slot}b", st)] = first, second
        put(f"d{slot}b", 2 + st, True, gate(slot, 2 + st, True) * second)

    def backward_middle(slot):
        take_back(f"d{slot}b")
        for st in STREAMS:
            b = 2 + st
            step = back_norm(
                vals[at(f"k{slot}b", st)], held_inv(slot, "b", st), gain(b, True), got(f"d{slot}b", b, True)
            )
            inner = vals[at(f"d{slot}a", st)] + mix(overlaps[over_at(slot, b, True)], step)
            put(f"d{slot}a", b, False, gate(slot, b, False) * inner)
            vals[at(f"d{slot}b", st)] = vals[at(f"d{slot}b", st)] + step
            vals[at(f"d{slot}a", st)] = inner
        send_out(f"d{slot}a")

    def backward_end(slot, st):
        b = 2 + st
        return vals[at(f"d{slot}a", st)] + back_norm(
            vals[at(f"k{slot}a", st)], held_inv(slot, "a", st), gain(b, False), got(f"d{slot}a", b, False)
        )

    def expert_forward(name):
        gp, up = inward((wgn, wun), name)
        outward((name,), ((activate(gp, up), wd),))

    def expert_backward(name, pres):
        act, = inward((wdn,), name)
        backward(name, act, *pre_at(pres))

    def ready_unit(u):
        last = 1 if u < 2 else 0
        wait_bulk(u)
        arrive_if(helds[u])
        arrive_if(patches[u][1 - last])
        held = held_in[u].astype(F32)
        both = both_picks(1, u)
        keep = 1.0 - jnp.sum(held, axis=0, keepdims=True)
        parts = [mm_t(both.astype(BF), held[i * width:(i + 1) * width].astype(BF)) for i in range(2)]
        moves[u] = parts[last]
        fresh_base[u] = mm((both * keep).astype(BF), base[u]) + mm(parts[1 - last].astype(BF), patch_in[u, 1 - last])

    def pick_new(u):
        last = 1 if u < 2 else 0
        arrive_if(patches[u][last])
        return fresh_base[u] + mm(moves[u].astype(BF), patch_in[u, last])

    def settle(u, parts):
        new_sel = last_picks(1, u)
        fresh = 1.0 - jnp.sum(new_sel, axis=0, keepdims=True)
        old_sel = held_in[u].astype(F32) * fresh
        kept = eye * (fresh - jnp.sum(old_sel, axis=0, keepdims=True))
        picks = [old_sel] + [new_sel[i * width:(i + 1) * width] for i, _ in parts]
        rows = [patch_in[u, i].astype(F32) for i in range(2)] + [value for _, value in parts]
        spread = mm_t(eye.astype(BF), jnp.concatenate(picks).astype(BF))
        final[u] = (
            mm(kept.astype(BF), base[u]) + mm(spread.astype(BF), jnp.concatenate(rows).astype(BF))
        ).astype(BF)
        if u >= 2:
            spread_out[u - 2] = mm_t(eye.astype(BF), new_sel[:width].astype(BF)).astype(BF)

    def drain(buffer, i):
        sent = buffer.at[:, :, pl.ds(0, group - 1)]
        pltpu.make_async_copy(sent, sent, send_sem.at[i]).wait()

    small_copies[2].wait()
    start_kept(0)
    send_out("k0a")
    state_copies[0].wait()
    for st in STREAMS:
        both = pick(0, st, state[st])
        forward_start(0, st, both[:width], both[width:])
    send_out("f00")
    start_kept(1)
    send_out("k1a")
    state_copies[1].wait()
    for st in STREAMS:
        both = pick(0, 2 + st, state[2 + st])
        backward_start(0, st, both[:width], both[width:])
    send_out("d0b")

    for u in range(4):
        held_out[u] = last_picks(0, u).astype(BF)
    for u in range(4):
        start_if(helds[u])

        @pl.when(jnp.logical_not(helds[u][1]))
        def _(u=u):
            patch_in[u] = jnp.zeros(patch_in.shape[1:], BF)
            held_in[u] = jnp.zeros(held_in.shape[1:], BF)
    for slot in range(2):
        for u in range(4):
            overlaps[over_at(slot, u, False)] = crossing(slot, u, False)
            if u >= 2:
                overlaps[over_at(slot, u, True)] = crossing(slot, u, True)

    def wait_weight(i):
        if i < 3:
            weight_copies[i].wait()
        pair_copies[i].wait_recv()

    wait_weight(0)
    turn(wg, wgn)
    for hf in range(CUTS_OUT):
        take_out("k0a", hf)
    rows = jnp.concatenate([rows_of(hf, "k0a") for hf in range(CUTS_OUT)], axis=1)
    pre[0] = mm(rows, wgn[...])
    wait_weight(1)
    turn(wu, wun)
    pre[1] = mm(rows, wun[...])
    gp, up = pre_at("k0a")
    outward(("k0a",), ((activate(gp, up), wd),), wait_weight)
    expert_forward("f00")
    middle_kept(0)
    turn(wd, wdn)
    early[...], = inward((wdn,), "d0b")
    gp, up = inward((wgn, wun), "k0b")
    backward("d0b", early[...], gp, up)
    forward_middle(0)
    for st in STREAMS:
        send_patch(st, 0, vals[at("fx1", st)])
    backward_middle(0)
    for st in STREAMS:
        send_patch(2 + st, 1, vals[at("d0b", st)])
    gp, up = inward((wgn, wun), "f01", "k1a")
    outward(("f01", "k1a"), ((activate(gp, up), wd),))
    keep_pre("k1a", (gp[gr:], up[gr:]))
    expert_backward("d0a", "k0a")
    take_back("f01")
    for st in STREAMS:
        send_patch(st, 1, forward_end(0, st))
    for st in STREAMS:
        ready_unit(2 + st)
    middle_kept(1)
    take_back("d0a")
    for st in STREAMS:
        send_patch(2 + st, 0, backward_end(0, st))
    for st in STREAMS:
        ready_unit(st)
    for st in STREAMS:
        both = pick_new(st)
        forward_start(1, st, both[:width], both[width:])
    send_out("f10")
    for st in STREAMS:
        both = pick_new(2 + st)
        backward_start(1, st, both[:width], both[width:])
    send_out("d1b")
    gp, up = inward((wgn, wun), "f10", "k1b")
    outward(("f10",), ((activate(gp[:gr], up[:gr]), wd),))
    keep_pre("k1b", (gp[gr:], up[gr:]))
    expert_backward("d1b", "k1b")
    forward_middle(1)
    backward_middle(1)
    expert_forward("f11")
    expert_backward("d1a", "k1a")
    for st in STREAMS:
        settle(2 + st, [(1, vals[at("d1b", st)])])
    take_back("f11")
    for st in STREAMS:
        settle(st, [(0, vals[at("fx1", st)]), (1, forward_end(1, st))])
    drain(ins, 0)
    drain(bins.at[pl.ds(0, len(BACK) - 1)], 1)
    for copy in pair_copies:
        copy.wait_send()
    for goes, way in ((has_up, 0), (has_down, 1)):
        @pl.when(goes)
        def _(way=way):
            pairs = (base.at[pl.ds(0, 2)], patch_in.at[0], patch_in.at[0], held_in.at[pl.ds(0, 2)])
            for kind, sent in enumerate(pairs):
                pltpu.make_async_copy(sent, sent, relay_send.at[kind, way]).wait()
    take_back("d1a")
    for st in STREAMS:
        rows_out[st] = backward_end(1, st).astype(BF)
    drain(bins.at[pl.ds(0, 1)], 2)


def merge(final, rows, spread, out, merged, out_sem):
    units = final.shape[0]
    sources = [final.at[u] if u < 2 else merged.at[u - 2] for u in range(units)]
    copies = [pltpu.make_async_copy(sources[u], out.at[u], out_sem.at[u]) for u in range(units)]
    for u in range(units):
        if u >= 2:
            merged[u - 2] = (final[u].astype(F32) + mm(spread[u - 2], rows[u - 2])).astype(BF)
        copies[u].start()
    for copy in copies:
        copy.wait()


def stay(value):
    return pltpu.with_memory_space_constraint(value, pltpu.HBM)


def local(sizes, state_in, entering, saved, route_ids, gate_vals, w_gate, w_up, w_down, gains):
    ns, ne, nd = sizes
    group, width = ne * nd // 2, ne // 2 * CAP
    units, tokens, model = state_in.shape[1:]
    hidden = w_gate.shape[-1]
    tables = route_ids.shape[1] * route_ids.shape[2] * route_ids.shape[3]
    topk = route_ids.shape[-1]
    turn = (0, 1, 2, 5, 3, 4)
    ids = jnp.transpose(route_ids, turn).reshape(tables * topk, tokens)
    gates = jnp.transpose(gate_vals, turn).reshape(tables * topk, tokens)
    vmem = pl.BlockSpec(memory_space=pltpu.VMEM)
    anywhere = pl.BlockSpec(memory_space=pl.ANY)
    dma = pltpu.SemaphoreType.DMA
    scratch = [
        pltpu.VMEM((len(OUT), CUTS_OUT, ne, CAP, model // CUTS_OUT), BF),
        pltpu.VMEM((len(OUT), CUTS_OUT, group, CAP, model // CUTS_OUT), BF),
        pltpu.VMEM((len(BACK), CUTS_BACK, group, CAP, model // CUTS_BACK), BF),
        pltpu.VMEM((len(BACK), CUTS_BACK, group, CAP, model // CUTS_BACK), BF),
        pltpu.VMEM((units, tokens, model), BF),
        pltpu.VMEM(ids.shape, jnp.int32),
        pltpu.VMEM(gates.shape, F32),
        pltpu.VMEM(gains.shape[1:], F32),
        pltpu.VMEM((units, tokens, model), BF),
        pltpu.VMEM(saved.shape[1:], BF),
        pltpu.VMEM((units, 2, width, model), BF),
        pltpu.VMEM((units, 2, width, model), BF),
        pltpu.VMEM((units, 2 * width, tokens), BF),
        pltpu.VMEM((units, 2 * width, tokens), BF),
        pltpu.VMEM((tables, width, tokens), F32),
        pltpu.VMEM((tables, width, tokens), F32),
        pltpu.VMEM((12, width, 3 * width), F32),
        pltpu.VMEM((units, 2 * width, width), F32),
        pltpu.VMEM((units, 2 * width, model), F32),
        pltpu.VMEM((2 * len(VALS), width, model), F32),
        pltpu.VMEM((2 * len(INVS), width, tokens), F32),
        pltpu.VMEM((2 * len(PRES), group * CAP, 2 * hidden), F32),
        pltpu.VMEM((group * CAP, 2 * hidden), F32),
        pltpu.VMEM((2, 2 * group * CAP, 2 * hidden), F32),
        pltpu.VMEM((2 * hidden, model), BF),
        pltpu.VMEM((2 * hidden, model), BF),
        pltpu.VMEM((2 * hidden, model), BF),
        pltpu.VMEM((model, 2 * hidden), BF),
        pltpu.VMEM((model, 2 * hidden), BF),
        pltpu.VMEM((model, 2 * hidden), BF),
        dma((3,)), dma((len(OUT), CUTS_OUT)), dma((len(BACK),)),
        dma((4, 2)), dma((4, units)), dma((3,)),
        dma((2 + CUTS_BACK,)), dma((2 + CUTS_BACK,)), dma((4,)), dma((3,)),
    ]
    final, rows, spread = pl.pallas_call(
        functools.partial(kernel, sizes),
        out_shape=(
            jax.ShapeDtypeStruct((units, tokens, model), BF),
            jax.ShapeDtypeStruct((2, width, model), BF),
            jax.ShapeDtypeStruct((2, tokens, width), BF),
        ),
        in_specs=[anywhere] * 9,
        out_specs=(vmem, vmem, vmem),
        scratch_shapes=scratch,
        compiler_params=pltpu.CompilerParams(
            collective_id=0, has_side_effects=True, vmem_limit_bytes=46137344 if ne <= 4 else 67043328
        ),
    )(*map(stay, (
        state_in[0], entering[0], saved[0], ids, gates, jnp.swapaxes(w_gate[0, 0], 0, 1),
        jnp.swapaxes(w_up[0, 0], 0, 1), w_down[0, 0], gains[0],
    )))
    result = pl.pallas_call(
        merge,
        out_shape=jax.ShapeDtypeStruct((units, tokens, model), BF),
        in_specs=[vmem] * 3,
        out_specs=pl.BlockSpec(memory_space=pltpu.HBM),
        scratch_shapes=[
            pltpu.VMEM((units - 2, tokens, model), BF), dma((units,)),
        ],
        compiler_params=pltpu.CompilerParams(vmem_limit_bytes=8 * 1024 * 1024),
    )(final, rows, spread)
    return result[None]


def solution(mesh):
    in_specs = (
        P("segment", None, ("expert", "dp"), None),
        P(None, None, ("expert", "dp"), None),
        P("segment", None, None, ("expert", "dp"), None),
        P("segment", None, None, None, ("expert", "dp"), None),
        P("segment", None, None, None, ("expert", "dp"), None),
        P("segment", "expert", None, "dp"),
        P("segment", "expert", None, "dp"),
        P("segment", "expert", "dp", None),
        P("segment", None, None),
    )
    out_specs = P("segment", None, ("expert", "dp"), None)
    sizes = (mesh.shape["segment"], mesh.shape["expert"], mesh.shape["dp"])
    body = functools.partial(local, sizes)
    return jax.shard_map(body, mesh=mesh, in_specs=in_specs, out_specs=out_specs, check_vma=False)
```

```python
import functools
import jax
import jax.numpy as jnp
from jax import lax
from jax.experimental import pallas as pl
from jax.experimental.pallas import tpu as pltpu
from jax.sharding import PartitionSpec as P

CAP = 8
EPSILON = 1e-06
LAST = (((1,), (1,)), ((), ()))
MESH = pl.DeviceIdType.MESH
BF = jnp.bfloat16
F32 = jnp.float32
OUT = ("k0a", "f00", "d0b", "k1a", "k0b", "f01", "k1b", "d0a", "f10", "d1b", "f11", "d1a")
BACK = ("k0a", "f00", "k1a", "d0b", "f01", "d0a", "f10", "d1b", "f11", "d1a")
VALS = ("fx1", "fx2", "k0a", "k0b", "k1a", "k1b", "d0a", "d0b", "d1a", "d1b")
INVS = ("0a", "0b", "1a", "1b")
PRES = ("k0a", "k0b", "k1a", "k1b")
STREAMS = range(2)
CUTS_OUT = 2
CUTS_BACK = 2


def mm(a, b):
    return jnp.dot(a, b, preferred_element_type=F32)


def mm_t(a, b):
    return lax.dot_general(a, b, LAST, preferred_element_type=F32)


def mix(picks, rows):
    high = rows.astype(BF).astype(F32)
    rest = rows - high
    mid = rest.astype(BF).astype(F32)
    parts = jnp.concatenate([high, mid, rest - mid])
    return mm(picks.astype(BF), parts.astype(BF))


def unit_norm(rows, gain):
    inv = lax.rsqrt(jnp.mean(rows * rows, axis=-1, keepdims=True) + EPSILON)
    return rows * inv * gain, inv


def back_norm(rows, inv, gain, grad):
    weighted = gain * grad
    total = jnp.sum(weighted * rows, axis=-1, keepdims=True)
    return inv * weighted - rows * (inv * inv * inv) * total / rows.shape[-1]


def quotient(a, b):
    return a // b if isinstance(a, int) else lax.div(a, b)


def remainder(a, b):
    return a % b if isinstance(a, int) else lax.rem(a, b)


def kernel(sizes, state_in, entering, saved_in, ids_in, gates_in, wg_in, wu_in, wd_in, gains_in,
           final, rows_out, spread_out,
           outs, ins, bouts, bins, base, ids, gates, gains, state, saved, patch_out, patch_in, held_out, held_in,
           sel, gate_col, overlaps, moves, fresh_base, vals, invs, pre, early, hold, wg, wu, wd, wgn, wun, wdn,
           send_sem, recv_sem, back_sem, relay_send, relay_recv, weight_sem,
           pair_send, pair_recv, input_sem, small_sem):
    ns, ne, nd = sizes
    nh = nd // 2
    group = ne * nh
    ec = ne // 2
    width = ec * CAP
    tokens, model = state_in.shape[1], state_in.shape[2]
    hidden = wg_in.shape[0]
    ho, hb = model // CUTS_OUT, model // CUTS_BACK
    gr = group * CAP
    seg, ex, dp = lax.axis_index("segment"), lax.axis_index("expert"), lax.axis_index("dp")
    half, side = lax.div(dp, 2), lax.rem(dp, 2)
    me = ex * nh + half

    saved_copies = [pltpu.make_async_copy(saved_in.at[s], saved.at[s], input_sem.at[s]) for s in range(2)]
    state_copies = [
        pltpu.make_async_copy(state_in.at[pl.ds(2 * i, 2)], state.at[pl.ds(2 * i, 2)], input_sem.at[2 + i])
        for i in range(2)
    ]
    small_copies = [
        pltpu.make_async_copy(source, dest, small_sem.at[i])
        for i, (source, dest) in enumerate(((ids_in, ids), (gates_in, gates), (gains_in, gains)))
    ]
    for copy in (*small_copies, saved_copies[0]):
        copy.start()

    barrier = pltpu.get_barrier_semaphore()

    def each_peer(body):
        if group <= 8:
            for k in reversed(range(1, group)):
                body(k)
        else:
            pl.loop(1, group)(body)

    def peer(k):
        te = lax.rem(ex + quotient(k, nh), ne)
        th = lax.rem(half + remainder(k, nh), nh)
        return te, th, (seg, te, th * 2 + 1 - side)

    partner = (seg, ex, half * 2 + 1 - side)
    has_up, has_down = seg < ns - 1, seg > 0

    def greet(k):
        pl.semaphore_signal(barrier, inc=1, device_id=peer(k)[2], device_id_type=MESH)

    each_peer(greet)
    pl.semaphore_signal(barrier, inc=1, device_id=partner, device_id_type=MESH)

    @pl.when(has_up)
    def _():
        pl.semaphore_signal(barrier, inc=1, device_id=(seg + 1, ex, dp), device_id_type=MESH)

    @pl.when(has_down)
    def _():
        pl.semaphore_signal(barrier, inc=1, device_id=(seg - 1, ex, dp), device_id_type=MESH)

    weights = ((wg_in, wg), (wu_in, wu), (wd_in, wd))
    weight_copies = [
        pltpu.make_async_copy(source, dest.at[pl.ds(0, hidden)], weight_sem.at[i])
        for i, (source, dest) in enumerate(weights)
    ]
    pieces = [(source, dest.at[pl.ds(hidden, hidden)]) for source, dest in weights[:2]] + [
        (wd_in.at[:, pl.ds(hf * hb, hb)], wd.at[pl.ds(hidden, hidden), pl.ds(hf * hb, hb)]) for hf in range(CUTS_BACK)
    ]
    pair_copies = [
        pltpu.make_async_remote_copy(
            src_ref=source, dst_ref=dest, send_sem=pair_send.at[i],
            recv_sem=pair_recv.at[i], device_id=partner, device_id_type=MESH,
        )
        for i, (source, dest) in enumerate(pieces)
    ]
    for copy in (state_copies[0], *weight_copies, saved_copies[1], state_copies[1]):
        copy.start()

    neighbours = jnp.where(has_up, 1, 0) + jnp.where(has_down, 1, 0)
    pl.semaphore_wait(barrier, group + neighbours)
    for copy in pair_copies:
        copy.start()

    def relay(unit, kind, source, dest):
        up = unit in (0, 3)
        goes, comes = (has_up, has_down) if up else (has_down, has_up)
        target = lax.rem(seg + (1 if up else ns - 1), ns)
        copy = pltpu.make_async_remote_copy(
            src_ref=source, dst_ref=dest, send_sem=relay_send.at[kind, 0 if up else 1],
            recv_sem=relay_recv.at[kind, unit], device_id=(target, ex, dp), device_id_type=MESH,
        )
        return goes, comes, copy

    def start_if(triple):
        @pl.when(triple[0])
        def _():
            triple[2].start()

    def arrive_if(triple):
        @pl.when(triple[1])
        def _():
            triple[2].wait_recv()

    bulk = [relay(u, 0, state_in.at[u], base.at[u]) for u in range(4)]
    enter = [pltpu.make_async_copy(entering.at[u], base.at[u], relay_recv.at[0, u]) for u in range(4)]
    for u in range(4):
        start_if(bulk[u])

        @pl.when(jnp.logical_not(bulk[u][1]))
        def _(u=u):
            enter[u].start()

    units = state_in.shape[0]
    lane = lax.broadcasted_iota(jnp.int32, (tokens, tokens), 1)
    row = lax.broadcasted_iota(jnp.int32, (tokens, tokens), 0)
    before = (row < lane).astype(F32).astype(BF)
    eye = (row == lane).astype(F32)
    slot_row = lax.broadcasted_iota(jnp.int32, (CAP, tokens), 0).astype(F32)
    su = 2 * units
    topk = ids.shape[0] // (2 * su)

    def tab(slot, unit, sub):
        return sub * su + slot * units + unit

    small_copies[0].wait()
    small_copies[1].wait()
    for e in range(ec):
        routed, weight = [], []
        for j in range(2):
            count, total = jnp.zeros((su, tokens), F32), jnp.zeros((su, tokens), F32)
            for k in range(topk):
                rows = pl.ds(k * 2 + j, su, stride=2 * topk)
                match = ids[rows, :] == e
                count = count + match.astype(F32)
                total = total + jnp.where(match, gates[rows, :], 0.0)
            routed.append(count)
            weight.append(total)
        routed = jnp.concatenate(routed)
        weight = jnp.concatenate(weight)
        earlier = mm(routed.astype(BF), before)
        for tb in range(2 * su):
            hit = (routed[tb:tb + 1] == 1.0) & (earlier[tb:tb + 1] == slot_row)
            one = jnp.where(hit, 1.0, 0.0)
            sel[tb, e * CAP:(e + 1) * CAP] = one
            gate_col[tb, e * CAP:(e + 1) * CAP] = jnp.broadcast_to(
                jnp.sum(one * weight[tb:tb + 1], axis=1, keepdims=True), (CAP, tokens)
            )

    def first_second(slot, unit):
        first = unit % 2
        return sel[tab(slot, unit, first)], sel[tab(slot, unit, 1 - first)]

    def last_picks(slot, unit):
        s1, s2 = first_second(slot, unit)
        if unit < 2:
            s1 = s1 * (1.0 - jnp.sum(s2, axis=0, keepdims=True))
        else:
            s2 = s2 * (1.0 - jnp.sum(s1, axis=0, keepdims=True))
        return jnp.concatenate([s1, s2])

    def both_picks(slot, unit):
        return jnp.concatenate(first_second(slot, unit))

    def pick(slot, unit, values):
        return mm(both_picks(slot, unit).astype(BF), values)

    def gate(slot, unit, second):
        sub = 1 - unit % 2 if second else unit % 2
        return gate_col[tab(slot, unit, sub)][:, 0:1]

    def gain(unit, second):
        sub = 1 - unit % 2 if second else unit % 2
        return gains[sub:sub + 1]

    patches = [[relay(u, 1 + i, patch_out.at[u, i], patch_in.at[u, i]) for i in range(2)] for u in range(4)]
    helds = [relay(u, 3, held_out.at[u], held_in.at[u]) for u in range(4)]

    def wait_bulk(u):
        arrive_if(bulk[u])

        @pl.when(jnp.logical_not(bulk[u][1]))
        def _():
            enter[u].wait()

    def out_copy(name, hf, k):
        i = OUT.index(name)
        te, th, device = peer(k)
        return pltpu.make_async_remote_copy(
            src_ref=outs.at[i, hf, te], dst_ref=ins.at[i, hf, me], send_sem=send_sem.at[0],
            recv_sem=recv_sem.at[i, hf], device_id=device, device_id_type=MESH,
        )

    def back_copy(name, hf, k):
        i = BACK.index(name)
        te, th, device = peer(k)
        return pltpu.make_async_remote_copy(
            src_ref=bouts.at[i, hf, te * nh + th], dst_ref=bins.at[i, hf, me], send_sem=send_sem.at[1 if i + 1 < len(BACK) else 2],
            recv_sem=back_sem.at[i], device_id=device, device_id_type=MESH,
        )

    def send_out(name):
        i = OUT.index(name)
        for hf in range(CUTS_OUT):
            each_peer(lambda k, hf=hf: out_copy(name, hf, k).start())
        for hf in range(CUTS_OUT):
            pltpu.make_async_copy(outs.at[i, hf, ex], ins.at[i, hf, me], recv_sem.at[i, hf]).start()

    def send_back(name, hf):
        i = BACK.index(name)
        each_peer(lambda k: back_copy(name, hf, k).start())
        pltpu.make_async_copy(bouts.at[i, hf, me], bins.at[i, hf, me], back_sem.at[i]).start()

    def take_out(name, hf):
        i = OUT.index(name)
        pltpu.make_async_copy(ins.at[i, hf], ins.at[i, hf], recv_sem.at[i, hf]).wait()

    def take_back(name):
        i = BACK.index(name)
        pltpu.make_async_copy(bins.at[i], bins.at[i], back_sem.at[i]).wait()

    def put(name, unit, second, rows):
        j = 1 - unit % 2 if second else unit % 2
        for e in range(ec):
            for hf in range(CUTS_OUT):
                outs[OUT.index(name), hf, j * ec + e] = (
                    rows[e * CAP:(e + 1) * CAP, hf * ho:(hf + 1) * ho].astype(BF)
                )

    def got(name, unit, second):
        j = 1 - unit % 2 if second else unit % 2
        i = BACK.index(name)
        parts = []
        for e in range(ec):
            first = (j * ec + e) * nh
            halves = []
            for hf in range(CUTS_BACK):
                total = bins[i, hf, first].astype(F32)
                for q in range(1, nh):
                    total = total + bins[i, hf, first + q].astype(F32)
                halves.append(total)
            parts.append(jnp.concatenate(halves, axis=1))
        return parts[0] if ec == 1 else jnp.concatenate(parts)

    def rows_of(hf, *names):
        parts = [ins[OUT.index(name), hf].astype(F32).reshape(gr, ho) for name in names]
        return (parts[0] if len(parts) == 1 else jnp.concatenate(parts)).astype(BF)

    def give(name, hf, rows):
        bouts[BACK.index(name), hf] = rows.reshape(group, CAP, hb).astype(BF)

    def cut(weight, hf):
        return weight[:, hf * hb:(hf + 1) * hb]

    def turn(source, dest):
        for c in range(0, model, 256):
            dest[c:c + 256] = source[:, c:c + 256].T

    def inward(weights, *names):
        sums = []
        for hf in range(CUTS_OUT):
            for name in names:
                take_out(name, hf)
            rows = rows_of(hf, *names)
            for i, weight in enumerate(weights):
                part = mm(rows, weight[hf * ho:(hf + 1) * ho])
                if hf > 0:
                    part = part + hold[i, :len(names) * gr]
                if hf + 1 < CUTS_OUT:
                    hold[i, :len(names) * gr] = part
                else:
                    sums.append(part)
        return sums

    def activate(gp, up):
        return (gp * jax.nn.sigmoid(gp) * up).astype(BF)

    def outward(names, pairs, ready=None, later=()):
        for hf in range(CUTS_BACK):
            if ready is not None:
                ready(2 + hf)
            total = mm(pairs[0][0], cut(pairs[0][1], hf))
            for a, weight in pairs[1:]:
                total = total + mm(a, cut(weight, hf))
            for n, name in enumerate(names):
                give(name, hf, total[n * gr:(n + 1) * gr])
                if name not in later:
                    send_back(name, hf)

    def factors(gp, up):
        sig = jax.nn.sigmoid(gp)
        return up * sig * (1.0 + gp * (1.0 - sig)), gp * sig

    def backward(name, act, to_gate, to_up):
        outward((name,), (((act * to_gate).astype(BF), wg), ((act * to_up).astype(BF), wu)))

    def at(name, st):
        return VALS.index(name) * 2 + st

    def inv_at(slot, which, st):
        return INVS.index(f"{slot}{which}") * 2 + st

    def keep_inv(slot, which, st, inv):
        invs[inv_at(slot, which, st)] = jnp.broadcast_to(inv, (width, tokens))

    def held_inv(slot, which, st):
        return invs[inv_at(slot, which, st)][:, 0:1]

    def pre_at(name):
        i = PRES.index(name) * 2
        return pre[i], pre[i + 1]

    def keep_pre(name, values):
        i = PRES.index(name) * 2
        pre[i], pre[i + 1] = factors(*values)

    def crossing(slot, unit, transposed):
        s1, s2 = first_second(slot, unit)
        if transposed:
            s1, s2 = s2, s1
        return mm_t(s2.astype(BF), jnp.concatenate([s1, s1, s1]).astype(BF))

    def over_at(slot, unit, transposed):
        return slot * 6 + unit + (2 if transposed else 0)

    def start_kept(slot):
        name = f"k{slot}a"
        saved_copies[slot].wait()
        for st in STREAMS:
            b = 2 + st
            both = pick(slot, b, saved[slot, st])
            vals[at(f"k{slot}a", st)], vals[at(f"k{slot}b", st)] = both[:width], both[width:]
            rows, inv = unit_norm(both[:width], gain(b, False))
            put(name, b, False, rows)
            keep_inv(slot, "a", st, inv)

    def middle_kept(slot):
        take_back(f"k{slot}a")
        for st in STREAMS:
            b = 2 + st
            add = gate(slot, b, False) * got(f"k{slot}a", b, False)
            middle = vals[at(f"k{slot}b", st)] + mix(overlaps[over_at(slot, b, False)], add)
            vals[at(f"k{slot}b", st)] = middle
            rows, inv = unit_norm(middle, gain(b, True))
            put(f"k{slot}b", b, True, rows)
            keep_inv(slot, "b", st, inv)
        send_out(f"k{slot}b")

    def forward_start(slot, st, first, second):
        vals[at("fx1", st)], vals[at("fx2", st)] = first, second
        put(f"f{slot}0", st, False, unit_norm(first, gain(st, False))[0])

    def send_patch(u, part, rows):
        patch_out[u, part] = rows.astype(BF)
        start_if(patches[u][part])

    def forward_middle(slot):
        take_back(f"f{slot}0")
        for st in STREAMS:
            add = gate(slot, st, False) * got(f"f{slot}0", st, False)
            vals[at("fx1", st)] = vals[at("fx1", st)] + add
            middle = vals[at("fx2", st)] + mix(overlaps[over_at(slot, st, False)], add)
            vals[at("fx2", st)] = middle
            put(f"f{slot}1", st, True, unit_norm(middle, gain(st, True))[0])
        send_out(f"f{slot}1")

    def forward_end(slot, st):
        return vals[at("fx2", st)] + gate(slot, st, True) * got(f"f{slot}1", st, True)

    def backward_start(slot, st, first, second):
        vals[at(f"d{slot}a", st)], vals[at(f"d{slot}b", st)] = first, second
        put(f"d{slot}b", 2 + st, True, gate(slot, 2 + st, True) * second)

    def backward_middle(slot):
        take_back(f"d{slot}b")
        for st in STREAMS:
            b = 2 + st
            step = back_norm(
                vals[at(f"k{slot}b", st)], held_inv(slot, "b", st), gain(b, True), got(f"d{slot}b", b, True)
            )
            inner = vals[at(f"d{slot}a", st)] + mix(overlaps[over_at(slot, b, True)], step)
            put(f"d{slot}a", b, False, gate(slot, b, False) * inner)
            vals[at(f"d{slot}b", st)] = vals[at(f"d{slot}b", st)] + step
            vals[at(f"d{slot}a", st)] = inner
        send_out(f"d{slot}a")

    def backward_end(slot, st):
        b = 2 + st
        return vals[at(f"d{slot}a", st)] + back_norm(
            vals[at(f"k{slot}a", st)], held_inv(slot, "a", st), gain(b, False), got(f"d{slot}a", b, False)
        )

    def expert_forward(name):
        gp, up = inward((wgn, wun), name)
        outward((name,), ((activate(gp, up), wd),))

    def expert_backward(name, pres):
        act, = inward((wdn,), name)
        backward(name, act, *pre_at(pres))

    def ready_unit(u):
        last = 1 if u < 2 else 0
        wait_bulk(u)
        arrive_if(helds[u])
        arrive_if(patches[u][1 - last])
        held = held_in[u].astype(F32)
        both = both_picks(1, u)
        keep = 1.0 - jnp.sum(held, axis=0, keepdims=True)
        parts = [mm_t(both.astype(BF), held[i * width:(i + 1) * width].astype(BF)) for i in range(2)]
        moves[u] = parts[last]
        fresh_base[u] = mm((both * keep).astype(BF), base[u]) + mm(parts[1 - last].astype(BF), patch_in[u, 1 - last])

    def pick_new(u):
        last = 1 if u < 2 else 0
        arrive_if(patches[u][last])
        return fresh_base[u] + mm(moves[u].astype(BF), patch_in[u, last])

    def settle(u, parts):
        new_sel = last_picks(1, u)
        fresh = 1.0 - jnp.sum(new_sel, axis=0, keepdims=True)
        old_sel = held_in[u].astype(F32) * fresh
        kept = eye * (fresh - jnp.sum(old_sel, axis=0, keepdims=True))
        picks = [old_sel] + [new_sel[i * width:(i + 1) * width] for i, _ in parts]
        rows = [patch_in[u, i].astype(F32) for i in range(2)] + [value for _, value in parts]
        spread = mm_t(eye.astype(BF), jnp.concatenate(picks).astype(BF))
        final[u] = (
            mm(kept.astype(BF), base[u]) + mm(spread.astype(BF), jnp.concatenate(rows).astype(BF))
        ).astype(BF)
        if u >= 2:
            spread_out[u - 2] = mm_t(eye.astype(BF), new_sel[:width].astype(BF)).astype(BF)

    def drain(buffer, i):
        sent = buffer.at[:, :, pl.ds(0, group - 1)]
        pltpu.make_async_copy(sent, sent, send_sem.at[i]).wait()

    small_copies[2].wait()
    start_kept(0)
    send_out("k0a")
    state_copies[0].wait()
    for st in STREAMS:
        both = pick(0, st, state[st])
        forward_start(0, st, both[:width], both[width:])
    send_out("f00")
    start_kept(1)
    state_copies[1].wait()
    for st in STREAMS:
        both = pick(0, 2 + st, state[2 + st])
        backward_start(0, st, both[:width], both[width:])
    send_out("d0b")

    for u in range(4):
        held_out[u] = last_picks(0, u).astype(BF)
    for u in range(4):
        start_if(helds[u])

        @pl.when(jnp.logical_not(helds[u][1]))
        def _(u=u):
            patch_in[u] = jnp.zeros(patch_in.shape[1:], BF)
            held_in[u] = jnp.zeros(held_in.shape[1:], BF)
    for slot in range(2):
        for u in range(4):
            overlaps[over_at(slot, u, False)] = crossing(slot, u, False)
            if u >= 2:
                overlaps[over_at(slot, u, True)] = crossing(slot, u, True)

    def wait_weight(i):
        if i < 3:
            weight_copies[i].wait()
        pair_copies[i].wait_recv()

    wait_weight(0)
    turn(wg, wgn)
    for hf in range(CUTS_OUT):
        take_out("k0a", hf)
    rows = jnp.concatenate([rows_of(hf, "k0a") for hf in range(CUTS_OUT)], axis=1)
    gp = mm(rows, wgn[...])
    wait_weight(1)
    turn(wu, wun)
    up = mm(rows, wun[...])
    outward(("k0a",), ((activate(gp, up), wd),), wait_weight)
    keep_pre("k0a", (gp, up))
    expert_forward("f00")
    middle_kept(0)
    turn(wd, wdn)
    early[...], = inward((wdn,), "d0b")
    send_out("k1a")
    gp, up = inward((wgn, wun), "k0b")
    backward("d0b", early[...], *factors(gp, up))
    forward_middle(0)
    for st in STREAMS:
        send_patch(st, 0, vals[at("fx1", st)])
    backward_middle(0)
    for st in STREAMS:
        send_patch(2 + st, 1, vals[at("d0b", st)])
    gp, up = inward((wgn, wun), "f01", "k1a")
    outward(("f01", "k1a"), ((activate(gp, up), wd),), later=("k1a",))
    for hf in range(CUTS_BACK):
        send_back("k1a", hf)
    keep_pre("k1a", (gp[gr:], up[gr:]))
    expert_backward("d0a", "k0a")
    take_back("f01")
    for st in STREAMS:
        send_patch(st, 1, forward_end(0, st))
    for st in STREAMS:
        ready_unit(2 + st)
    middle_kept(1)
    take_back("d0a")
    for st in STREAMS:
        send_patch(2 + st, 0, backward_end(0, st))
    for st in STREAMS:
        ready_unit(st)
    for st in STREAMS:
        both = pick_new(st)
        forward_start(1, st, both[:width], both[width:])
    send_out("f10")
    for st in STREAMS:
        both = pick_new(2 + st)
        backward_start(1, st, both[:width], both[width:])
    send_out("d1b")
    gp, up = inward((wgn, wun), "f10", "k1b")
    outward(("f10",), ((activate(gp[:gr], up[:gr]), wd),))
    keep_pre("k1b", (gp[gr:], up[gr:]))
    expert_backward("d1b", "k1b")
    forward_middle(1)
    backward_middle(1)
    expert_forward("f11")
    expert_backward("d1a", "k1a")
    for st in STREAMS:
        settle(2 + st, [(1, vals[at("d1b", st)])])
    take_back("f11")
    for st in STREAMS:
        settle(st, [(0, vals[at("fx1", st)]), (1, forward_end(1, st))])
    drain(ins, 0)
    drain(bins.at[pl.ds(0, len(BACK) - 1)], 1)
    for copy in pair_copies:
        copy.wait_send()
    for goes, way in ((has_up, 0), (has_down, 1)):
        @pl.when(goes)
        def _(way=way):
            pairs = (base.at[pl.ds(0, 2)], patch_in.at[0], patch_in.at[0], held_in.at[pl.ds(0, 2)])
            for kind, sent in enumerate(pairs):
                pltpu.make_async_copy(sent, sent, relay_send.at[kind, way]).wait()
    take_back("d1a")
    for st in STREAMS:
        rows_out[st] = backward_end(1, st).astype(BF)
    drain(bins.at[pl.ds(0, 1)], 2)


def merge(final, rows, spread, out, merged, out_sem):
    units = final.shape[0]
    sources = [final.at[u] if u < 2 else merged.at[u - 2] for u in range(units)]
    copies = [pltpu.make_async_copy(sources[u], out.at[u], out_sem.at[u]) for u in range(units)]
    for u in range(units):
        if u >= 2:
            merged[u - 2] = (final[u].astype(F32) + mm(spread[u - 2], rows[u - 2])).astype(BF)
        copies[u].start()
    for copy in copies:
        copy.wait()


def stay(value):
    return pltpu.with_memory_space_constraint(value, pltpu.HBM)


def local(sizes, state_in, entering, saved, route_ids, gate_vals, w_gate, w_up, w_down, gains):
    ns, ne, nd = sizes
    group, width = ne * nd // 2, ne // 2 * CAP
    units, tokens, model = state_in.shape[1:]
    hidden = w_gate.shape[-1]
    tables = route_ids.shape[1] * route_ids.shape[2] * route_ids.shape[3]
    topk = route_ids.shape[-1]
    turn = (0, 1, 2, 5, 3, 4)
    ids = jnp.transpose(route_ids, turn).reshape(tables * topk, tokens)
    gates = jnp.transpose(gate_vals, turn).reshape(tables * topk, tokens)
    vmem = pl.BlockSpec(memory_space=pltpu.VMEM)
    anywhere = pl.BlockSpec(memory_space=pl.ANY)
    dma = pltpu.SemaphoreType.DMA
    scratch = [
        pltpu.VMEM((len(OUT), CUTS_OUT, ne, CAP, model // CUTS_OUT), BF),
        pltpu.VMEM((len(OUT), CUTS_OUT, group, CAP, model // CUTS_OUT), BF),
        pltpu.VMEM((len(BACK), CUTS_BACK, group, CAP, model // CUTS_BACK), BF),
        pltpu.VMEM((len(BACK), CUTS_BACK, group, CAP, model // CUTS_BACK), BF),
        pltpu.VMEM((units, tokens, model), BF),
        pltpu.VMEM(ids.shape, jnp.int32),
        pltpu.VMEM(gates.shape, F32),
        pltpu.VMEM(gains.shape[1:], F32),
        pltpu.VMEM((units, tokens, model), BF),
        pltpu.VMEM(saved.shape[1:], BF),
        pltpu.VMEM((units, 2, width, model), BF),
        pltpu.VMEM((units, 2, width, model), BF),
        pltpu.VMEM((units, 2 * width, tokens), BF),
        pltpu.VMEM((units, 2 * width, tokens), BF),
        pltpu.VMEM((tables, width, tokens), F32),
        pltpu.VMEM((tables, width, tokens), F32),
        pltpu.VMEM((12, width, 3 * width), F32),
        pltpu.VMEM((units, 2 * width, width), F32),
        pltpu.VMEM((units, 2 * width, model), F32),
        pltpu.VMEM((2 * len(VALS), width, model), F32),
        pltpu.VMEM((2 * len(INVS), width, tokens), F32),
        pltpu.VMEM((2 * len(PRES), group * CAP, 2 * hidden), F32),
        pltpu.VMEM((group * CAP, 2 * hidden), F32),
        pltpu.VMEM((2, 2 * group * CAP, 2 * hidden), F32),
        pltpu.VMEM((2 * hidden, model), BF),
        pltpu.VMEM((2 * hidden, model), BF),
        pltpu.VMEM((2 * hidden, model), BF),
        pltpu.VMEM((model, 2 * hidden), BF),
        pltpu.VMEM((model, 2 * hidden), BF),
        pltpu.VMEM((model, 2 * hidden), BF),
        dma((3,)), dma((len(OUT), CUTS_OUT)), dma((len(BACK),)),
        dma((4, 2)), dma((4, units)), dma((3,)),
        dma((2 + CUTS_BACK,)), dma((2 + CUTS_BACK,)), dma((4,)), dma((3,)),
    ]
    final, rows, spread = pl.pallas_call(
        functools.partial(kernel, sizes),
        out_shape=(
            jax.ShapeDtypeStruct((units, tokens, model), BF),
            jax.ShapeDtypeStruct((2, width, model), BF),
            jax.ShapeDtypeStruct((2, tokens, width), BF),
        ),
        in_specs=[anywhere] * 9,
        out_specs=(vmem, vmem, vmem),
        scratch_shapes=scratch,
        compiler_params=pltpu.CompilerParams(
            collective_id=0, has_side_effects=True, vmem_limit_bytes=46137344 if ne <= 4 else 67043328
        ),
    )(*map(stay, (
        state_in[0], entering[0], saved[0], ids, gates, jnp.swapaxes(w_gate[0, 0], 0, 1),
        jnp.swapaxes(w_up[0, 0], 0, 1), w_down[0, 0], gains[0],
    )))
    result = pl.pallas_call(
        merge,
        out_shape=jax.ShapeDtypeStruct((units, tokens, model), BF),
        in_specs=[vmem] * 3,
        out_specs=pl.BlockSpec(memory_space=pltpu.HBM),
        scratch_shapes=[
            pltpu.VMEM((units - 2, tokens, model), BF), dma((units,)),
        ],
        compiler_params=pltpu.CompilerParams(vmem_limit_bytes=8 * 1024 * 1024),
    )(final, rows, spread)
    return result[None]


def solution(mesh):
    in_specs = (
        P("segment", None, ("expert", "dp"), None),
        P(None, None, ("expert", "dp"), None),
        P("segment", None, None, ("expert", "dp"), None),
        P("segment", None, None, None, ("expert", "dp"), None),
        P("segment", None, None, None, ("expert", "dp"), None),
        P("segment", "expert", None, "dp"),
        P("segment", "expert", None, "dp"),
        P("segment", "expert", "dp", None),
        P("segment", None, None),
    )
    out_specs = P("segment", None, ("expert", "dp"), None)
    sizes = (mesh.shape["segment"], mesh.shape["expert"], mesh.shape["dp"])
    body = functools.partial(local, sizes)
    return jax.shard_map(body, mesh=mesh, in_specs=in_specs, out_specs=out_specs, check_vma=False)
```
